256 devices in a mesh: occ: 64 (over x_hi, y, z), off: 4 (over x_lo, core).
Axes of the slice: x: 4 (x_hi: 2, x_lo: 2; x = x_hi * 2 + x_lo), y: 4, z: 8, core: 2. Of those that a mesh axis runs over, the one named last changes fastest.
Arguments:
- factors: bfloat16 [64, 768, 2048], P('occ'), may hold values from -0.8984375 to 0.8984375
- occ_level: int32 [64], replicated, may hold values from 0 to 255
- vir_level: int32 [768], replicated, may hold values from 0 to 255
- occupied_energy_levels: float32 [256], replicated, may hold values from -2 to -0.5
- vir_table: float32 [256], replicated, may hold values from 0.5 to 4
- virtual_coefficient_matrix: bfloat16 [768, 1024], replicated, may hold values from -0.21875 to 0.21875
Outputs:
- density_ao: float32 [64, 2048, 1024], P(None, ('occ', 'off'))
The draws below stay inside these ranges and needn't reach their ends.
Inputs may be any that keep to these rules, and one draw needn't show every extreme that they name: `occ_level`: indices into occupied_energy_levels. `vir_level`: indices into vir_table.
All inputs are finite; a program needn't handle non-finite values.
Results may differ from the reference program's by a relative error of at most 0.0032.
Values may be sent and summed in bfloat16 or wider, within the bound.
No kernel may reach another device: no remote copies, remote signals or barrier semaphores. Data moves between devices by JAX's collectives and lax.ppermute only.
A program may use at most 64 MiB of HBM per device.

```python
import jax
import jax.numpy as jnp
from jax import lax

V = 768
NAUX = 2048
NORB = 1024
LEVELS = 256
PAIR_STEPS = 2
NOCC = 64
N_OFF = 4


def set_ends(result, rng, low, high):
    longest = result.shape.index(max(result.shape))
    spots = []
    for shift in (0, 1):
        where = [jax.random.randint(jax.random.fold_in(rng, axis), (), 0, length) for axis, length in enumerate(result.shape)]
        where[longest] = (where[longest] + shift) % result.shape[longest]
        spots.append(tuple(where))
    return result.at[spots[0]].set(low).at[spots[1]].set(high)


def level_of(own_key, extent, pieces, least, largest):
    loudness = 1.0
    for axis_at, blocks in pieces:
        steps = jax.random.uniform(jax.random.fold_in(jax.random.fold_in(own_key, 6), axis_at), (blocks,), jnp.float32, least / len(pieces), largest / len(pieces))
        loudness = loudness * jnp.repeat(jnp.exp(steps), extent[axis_at] // blocks).reshape((-1,) + (1,) * (len(extent) - 1 - axis_at))
    return loudness


def bell_draw(own_key, extent, scale, limit, cuts=(), kind=jnp.bfloat16):
    entries = scale * jax.random.normal(own_key, extent, jnp.float32)
    if cuts:
        entries = entries * level_of(own_key, extent, cuts, -0.22, 0.18)
    return jnp.clip(entries, -limit, limit).astype(kind)


def setup_inputs(seed: int = 0) -> dict:
    key_of = jax.random.split(jax.random.key(seed), 7)
    return {
        "factors": bell_draw(key_of[0], (NOCC, V, NAUX), 0.15, 0.8984375, ((0, 64),)),
        "occ_level": set_ends(jax.random.randint(key_of[1], (NOCC,), 0, LEVELS), jax.random.fold_in(key_of[1], 1), 0, LEVELS - 1).astype(jnp.int32),
        "vir_level": set_ends(jax.random.randint(key_of[2], (V,), 0, LEVELS), jax.random.fold_in(key_of[2], 1), 0, LEVELS - 1).astype(jnp.int32),
        "occupied_energy_levels": jnp.clip(jax.random.uniform(key_of[3], (LEVELS,), jnp.float32, -2.0, -0.5), -2.0, -0.5),
        "vir_table": jnp.clip(jax.random.uniform(key_of[4], (LEVELS,), jnp.float32, 0.5, 4.0), 0.5, 4.0),
        "virtual_coefficient_matrix": bell_draw(key_of[5], (V, NORB), V ** -0.5, 0.21875),
    }


def reference(factors, occ_level, vir_level, occupied_energy_levels, vir_table, virtual_coefficient_matrix):
    occ_energy = occupied_energy_levels[occ_level]
    vir_energy = vir_table[vir_level]
    offsets = N_OFF * PAIR_STEPS

    def one_orbital(orbital):
        own = lax.dynamic_index_in_dim(factors, orbital, 0, keepdims=False)
        own_energy = lax.dynamic_index_in_dim(occ_energy, orbital, 0, keepdims=False)

        def append_pair_term(offset, acc):
            pair_companion = ((orbital - offset.astype(jnp.int32)) % NOCC).astype(jnp.int32)
            other = lax.dynamic_index_in_dim(factors, pair_companion, 0, keepdims=False)
            other_energy = lax.dynamic_index_in_dim(occ_energy, pair_companion, 0, keepdims=False)
            integral = lax.dot_general(own, other, (((1,), (1,)), ((), ())), preferred_element_type=jnp.float32)
            denom = vir_energy[:, None] + vir_energy[None, :] - own_energy - other_energy
            amp = integral / denom
            pair_weight = (2.0 * amp - amp.T).astype(jnp.bfloat16)
            return acc + lax.dot_general(other, pair_weight, (((0,), (1,)), ((), ())), preferred_element_type=jnp.float32)

        gamma = lax.fori_loop(0, offsets, append_pair_term, jnp.zeros((NAUX, V), jnp.float32))
        lower_gamma_part = gamma.astype(jnp.bfloat16)
        return jnp.dot(lower_gamma_part, virtual_coefficient_matrix, preferred_element_type=jnp.float32)

    return lax.map(one_orbital, jnp.arange(NOCC, dtype=jnp.int32))
```

```python
import jax
import jax.numpy as jnp
from jax import lax
from jax.sharding import PartitionSpec as P

BOTH = ("occ", "off")


def lookup(level, table):
    hits = level[:, None] == jnp.arange(table.shape[0], dtype=jnp.int32)[None, :]
    return jnp.sum(jnp.where(hits, table[None, :], jnp.float32(0.0)), axis=1)


def moves(n_occ, rule):
    pairs = []
    for i in range(n_occ):
        for chip in range(2):
            for core in range(2):
                shift, to = rule(core)
                pairs.append((i * 4 + chip * 2 + core, ((i + shift) % n_occ) * 4 + chip * 2 + to))
    return pairs


def swap(n_occ, mask):
    return [(i * 4 + o, i * 4 + (o ^ mask)) for i in range(n_occ) for o in range(4)]


def body(
    factors, occ_level, vir_level, occupied_energy_levels, vir_table, virtual_coefficient_matrix
):
    n_occ = lax.axis_size("occ")
    occ_index = lax.axis_index("occ")
    off_index = lax.axis_index("off")
    chip = off_index // 2
    core = off_index % 2
    own = factors[0]
    n_vir, n_aux = own.shape
    half = n_vir // 2
    quarter = n_vir // 4

    ev = lookup(vir_level, vir_table)
    eo = lookup(occ_level, occupied_energy_levels)
    eo_i = lax.dynamic_index_in_dim(eo, occ_index, 0, keepdims=False)

    def eo_at(k):
        return lax.dynamic_index_in_dim(eo, (occ_index - k) % n_occ, 0, keepdims=False)

    x0 = lax.dynamic_slice_in_dim(own, chip * half, half, 0)
    x1 = lax.ppermute(x0, BOTH, moves(n_occ, lambda r: (1, 1) if r == 0 else (7, 0)))
    x2 = lax.ppermute(x1, BOTH, moves(n_occ, lambda r: (1, 0) if r == 1 else (-1, 1)))
    x3 = lax.ppermute(x2, BOTH, moves(n_occ, lambda r: (1, 1) if r == 0 else (-1, 0)))
    x3q = lax.dynamic_slice_in_dim(x3, (1 - core) * quarter, quarter, 0)
    x4 = lax.ppermute(x3q, BOTH, moves(n_occ, lambda r: (1, 1) if r == 1 else (-1, 0)))

    def amp_t(x, k, first):
        integral = lax.dot_general(x, own, (((1,), (1,)), ((), ())), preferred_element_type=jnp.float32)
        eb = lax.dynamic_slice_in_dim(ev, first, x.shape[0], 0)
        return integral / (eb[:, None] + ev[None, :] - eo_i - eo_at(k))

    def add(total, x, w):
        term = lax.dot_general(x, w, (((0,), (0,)), ((), ())), preferred_element_type=jnp.float32)
        return term if total is None else total + term

    first = chip * half + (1 - core) * quarter
    xq = lax.dynamic_slice_in_dim(own, first, quarter, 0)
    total = add(None, xq, amp_t(xq, 0, first).astype(jnp.bfloat16))

    for x, k in ((x1, jnp.where(core == 1, 1, 7)), (x2, jnp.where(core == 1, 6, 2)), (x3, jnp.where(core == 1, 3, 5))):
        at = amp_t(x, k, chip * half)
        mine = lax.dynamic_slice_in_dim(at, chip * half, half, 1)
        theirs = lax.dynamic_slice_in_dim(at, (1 - chip) * half, half, 1)
        got = lax.ppermute(theirs, BOTH, swap(n_occ, 2))
        low = jnp.where(chip == 0, mine, got)
        high = jnp.where(chip == 0, got, mine)
        back = jnp.concatenate([low.T, high.T], axis=1)
        total = add(total, x, (2.0 * at - back).astype(jnp.bfloat16))

    at = amp_t(x4, 4, first)
    piece = chip * 2 + (1 - core)
    back = jnp.zeros_like(at)
    for mask in range(4):
        target = piece ^ mask
        part = lax.dynamic_slice_in_dim(at, target * quarter, quarter, 1)
        if mask:
            part = lax.ppermute(part, BOTH, swap(n_occ, mask))
        back = lax.dynamic_update_slice_in_dim(back, part.T, target * quarter, 1)
    total = add(total, x4, (2.0 * at - back).astype(jnp.bfloat16))

    rows = n_aux // (n_occ * 4)
    blocks = total.reshape(n_occ, 2, 2, rows, n_vir)
    keep = lax.dynamic_index_in_dim(blocks, core, 2, keepdims=False)
    send = lax.dynamic_index_in_dim(blocks, 1 - core, 2, keepdims=False)
    both = keep + lax.ppermute(send, BOTH, swap(n_occ, 1))
    keep = lax.dynamic_index_in_dim(both, chip, 1, keepdims=False)
    send = lax.dynamic_index_in_dim(both, 1 - chip, 1, keepdims=False)
    gamma = keep + lax.ppermute(send, BOTH, swap(n_occ, 2))
    low = gamma.astype(jnp.bfloat16)
    mine = lax.all_to_all(low, "occ", split_axis=0, concat_axis=0, tiled=True)
    return jnp.einsum("sbd,dw->sbw", mine, virtual_coefficient_matrix, preferred_element_type=jnp.float32)


def solution(mesh):
    in_specs = (P("occ", None, None), P(), P(), P(), P(), P())
    out_specs = P(None, ("occ", "off"), None)
    return jax.shard_map(body, mesh=mesh, in_specs=in_specs, out_specs=out_specs, check_vma=False)
```

```python
import functools

import jax
import jax.numpy as jnp
from jax import lax
from jax.experimental import pallas as pl
from jax.experimental.pallas import tpu as pltpu
from jax.sharding import PartitionSpec as P

BOTH = ("occ", "off")
F32 = jnp.float32
BF16 = jnp.bfloat16
RING = 8
TN = (((0,), (0,)), ((), ()))
NT = (((1,), (1,)), ((), ()))


def lookup(level, table):
    hits = level[:, None] == jnp.arange(table.shape[0], dtype=jnp.int32)[None, :]
    return jnp.sum(jnp.where(hits, table[None, :], jnp.float32(0.0)), axis=1)


def moves(n_occ, rule):
    pairs = []
    half = n_occ // 2
    for i in range(n_occ):
        for chip in range(2):
            for core in range(2):
                j, to = rule(i, core)
                j %= n_occ
                flip = (i // half) ^ (j // half)
                pairs.append((i * 4 + chip * 2 + core, j * 4 + (chip ^ flip) * 2 + to))
    return pairs


def swap(n_occ, mask):
    return [(i * 4 + o, i * 4 + (o ^ mask)) for i in range(n_occ) for o in range(4)]


def round1(i, core):
    if core == 0:
        return i + 1, 1
    return (i + RING, 0) if i % RING else (i, 0)


def round2(i, core):
    if core == 1:
        return i + 1, 0
    return i - i % RING + (i - 1) % RING, 1


def round3(i, core):
    return (i + 1, 1) if core == 0 else (i - 1, 0)


def round4(i, core):
    return (i + 1, 0) if core == 1 else (i - 1, 1)


def sds(shape, dtype):
    return jax.ShapeDtypeStruct(shape, dtype)


def cost(flops, nbytes):
    return pl.CostEstimate(flops=flops, bytes_accessed=nbytes, transcendentals=0)


def amp_kernel(sc, own, x, evc, evr, eo, s_out, w_out, acc, *, half, steps, slot):
    t = pl.program_id(0)
    prod = lax.dot_general(x[...], own[...], NT, preferred_element_type=F32)

    @pl.when(t == 0)
    def _():
        acc[...] = prod

    @pl.when(t > 0)
    def _():
        acc[...] += prod

    @pl.when(t == steps - 1)
    def _():
        h = sc[0]
        e = jnp.concatenate([evc[...]] * (half // 128), axis=1)

        def amp(first):
            cols = pl.ds(pl.multiple_of(first * half, half), half)
            return acc[:, cols] / (e + evr[:, cols] - eo[sc[3]] - eo[sc[4 + slot]])

        s_out[...] = amp(1 - h).astype(s_out.dtype)
        mine = amp(h)
        w_out[...] = (2.0 * mine - mine.T).astype(BF16)


def mix_kernel(sc, s, q, w, o, *, half):
    h = sc[0]
    o[:, pl.ds(pl.multiple_of(h * half, half), half)] = w[...]
    other = 2.0 * s[...].astype(F32) - q[...].astype(F32).T
    o[:, pl.ds(pl.multiple_of((1 - h) * half, half), half)] = other.astype(BF16)


def gamma_kernel(*refs, n, half):
    xs, ws, outs = refs[:n], refs[n : 2 * n], refs[2 * n :]
    res = lax.dot_general(xs[0][...], ws[0][...], TN, preferred_element_type=F32)
    for k in range(1, n):
        res += lax.dot_general(xs[k][...], ws[k][...], TN, preferred_element_type=F32)
    outs[0][...] = res[:, :half]
    outs[1][...] = res[:, half:]


def last_kernel(sc, *refs, n):
    xs, ws, early, keep, send = refs[:n], refs[n : 2 * n], refs[2 * n], refs[2 * n + 1], refs[2 * n + 2]
    res = early[...]
    for k in range(n):
        res += lax.dot_general(xs[k][...], ws[k][...], TN, preferred_element_type=F32)
    res = res.reshape(res.shape[0] // 32, 2, 2, 8, res.shape[1])
    a, b = res[:, :, 0], res[:, :, 1]
    first = sc[1] == 0
    keep[...] = jnp.where(first, a, b)
    send[...] = jnp.where(first, b, a)


def body(
    factors, occ_level, vir_level, occupied_energy_levels, vir_table, virtual_coefficient_matrix
):
    n_occ = lax.axis_size("occ")
    occ_index = lax.axis_index("occ")
    off_index = lax.axis_index("off")
    chip = off_index // 2
    core = off_index % 2
    own = factors[0]
    n_vir, n_aux = own.shape
    half = n_vir // 2
    h = chip ^ (occ_index // (n_occ // 2))
    partners = [(occ_index - jnp.where(core == 0, a, b)) % n_occ for a, b in ((0, 1), (2, 7), (6, 3), (4, 5))]
    sc = jnp.stack([h, core, chip, occ_index, *partners]).astype(jnp.int32)

    x0 = lax.dynamic_slice_in_dim(own, h * half, half, 0)
    x1 = lax.ppermute(x0, BOTH, moves(n_occ, round1))
    x2 = lax.ppermute(x1, BOTH, moves(n_occ, round2))

    ev = lookup(vir_level, vir_table)
    eo = lookup(occ_level, occupied_energy_levels)
    evr = ev[None, :]
    evc = jnp.broadcast_to(lax.dynamic_slice_in_dim(ev, h * half, half, 0)[:, None], (half, 128))

    steps = 2
    tile = n_aux // steps

    def amp(x, slot, s_dtype):
        return pl.pallas_call(
            functools.partial(amp_kernel, half=half, steps=steps, slot=slot),
            out_shape=(sds((half, half), s_dtype), sds((half, half), BF16)),
            grid_spec=pltpu.PrefetchScalarGridSpec(
                num_scalar_prefetch=1,
                grid=(steps,),
                in_specs=[
                    pl.BlockSpec((n_vir, tile), lambda t, s: (0, t)),
                    pl.BlockSpec((half, tile), lambda t, s: (0, t)),
                    pl.BlockSpec((half, 128), lambda t, s: (0, 0)),
                    pl.BlockSpec((1, n_vir), lambda t, s: (0, 0)),
                    pl.BlockSpec(memory_space=pltpu.SMEM),
                ],
                out_specs=[pl.BlockSpec((half, half), lambda t, s: (0, 0))] * 2,
                scratch_shapes=[pltpu.VMEM((half, n_vir), F32)],
            ),
            cost_estimate=cost(2 * n_vir * half * n_aux, 2 * n_aux * (n_vir + half)),
            name="amp",
        )(sc, own, x, evc, evr, eo)

    def mix(s, w):
        q = lax.ppermute(s, BOTH, swap(n_occ, 2))
        whole = pl.BlockSpec((half, half), lambda t, s: (0, 0))
        return pl.pallas_call(
            functools.partial(mix_kernel, half=half),
            out_shape=sds((half, n_vir), BF16),
            grid_spec=pltpu.PrefetchScalarGridSpec(
                num_scalar_prefetch=1,
                grid=(1,),
                in_specs=[whole] * 3,
                out_specs=pl.BlockSpec((half, n_vir), lambda t, s: (0, 0)),
            ),
            cost_estimate=cost(half * half * 4, half * half * 14),
            name="mix",
        )(sc, s, q, w)

    y1 = jnp.where(core == 0, x0, x1)
    s1, v1 = amp(y1, 0, F32)
    x2, s1 = lax.optimization_barrier((x2, s1))
    x3 = lax.ppermute(x2, BOTH, moves(n_occ, round3))
    s2, v2 = amp(x2, 1, F32)
    w1 = mix(s1, v1)
    x3, s2, w1 = lax.optimization_barrier((x3, s2, w1))
    x4 = lax.ppermute(x3, BOTH, moves(n_occ, round4))
    s3, v3 = amp(x3, 2, F32)
    w2 = mix(s2, v2)

    tiles = 4
    tile_p = n_aux // tiles
    early = pl.pallas_call(
        functools.partial(gamma_kernel, n=2, half=half),
        out_shape=(sds((n_aux, half), F32),) * 2,
        grid=(tiles,),
        in_specs=[pl.BlockSpec((half, tile_p), lambda t: (0, t))] * 2
        + [pl.BlockSpec((half, n_vir), lambda t: (0, 0))] * 2,
        out_specs=[pl.BlockSpec((tile_p, half), lambda t: (t, 0))] * 2,
        cost_estimate=cost(4 * n_aux * half * n_vir, 4 * n_aux * half + 4 * n_aux * n_vir),
        name="gamma",
    )(y1, x2, w1, w2)
    x4, s3, early = lax.optimization_barrier((x4, s3, early))
    s4, v4 = amp(x4, 3, BF16)
    w3 = mix(s3, v3)
    w4 = mix(s4, v4)

    groups = tile_p // 32

    def last(g, early):
        return pl.pallas_call(
            functools.partial(last_kernel, n=2),
            out_shape=(sds((n_occ, 2, 8, half), F32),) * 2,
            grid_spec=pltpu.PrefetchScalarGridSpec(
                num_scalar_prefetch=1,
                grid=(tiles,),
                in_specs=[pl.BlockSpec((half, tile_p), lambda t, s: (0, t))] * 2
                + [pl.BlockSpec((half, half), lambda t, s: (0, g))] * 2
                + [pl.BlockSpec((tile_p, half), lambda t, s: (t, 0))],
                out_specs=[pl.BlockSpec((groups, 2, 8, half), lambda t, s: (t, 0, 0, 0))] * 2,
            ),
            cost_estimate=cost(2 * n_aux * half * n_vir, 4 * n_aux * (n_vir + half)),
            name="last",
        )(sc, x3, x4, w3, w4, early)

    def part(keep, got, c):
        a = lax.dynamic_index_in_dim(keep, c, 1, keepdims=False)
        return a + lax.dynamic_index_in_dim(got, c, 1, keepdims=False)

    def finish(g, keep, got, far):
        low = (part(keep, got, chip) + far.astype(F32)).astype(BF16)
        mine = lax.all_to_all(low, "occ", split_axis=0, concat_axis=0, tiled=True)
        c = virtual_coefficient_matrix[g * half : (g + 1) * half]
        return jnp.einsum("sbd,dw->sbw", mine, c, preferred_element_type=F32)

    keep0, send0 = last(0, early[0])
    early1, send0 = lax.optimization_barrier((early[1], send0))
    got0 = lax.ppermute(send0, BOTH, swap(n_occ, 1))
    keep1, send1 = last(1, early1)
    away0 = part(keep0, got0, 1 - chip).astype(BF16)
    away0, send1 = lax.optimization_barrier((away0, send1))
    far0 = lax.ppermute(away0, BOTH, swap(n_occ, 2))
    got1 = lax.ppermute(send1, BOTH, swap(n_occ, 1))
    away1 = part(keep1, got1, 1 - chip)
    away1, far0 = lax.optimization_barrier((away1, far0))
    far1 = lax.ppermute(away1, BOTH, swap(n_occ, 2))
    return finish(0, keep0, got0, far0) + finish(1, keep1, got1, far1)


def solution(mesh):
    in_specs = (P("occ", None, None), P(), P(), P(), P(), P())
    out_specs = P(None, ("occ", "off"), None)
    return jax.shard_map(body, mesh=mesh, in_specs=in_specs, out_specs=out_specs, check_vma=False)
```

```python
import functools

import jax
import jax.numpy as jnp
from jax import lax
from jax.experimental import pallas as pl
from jax.experimental.pallas import tpu as pltpu
from jax.sharding import PartitionSpec as P


BOTH = ("occ", "off")
F32 = jnp.float32
BF16 = jnp.bfloat16
RING = 8
TN = (((0,), (0,)), ((), ()))
NT = (((1,), (1,)), ((), ()))


def lookup(level, table):
    hits = level[:, None] == jnp.arange(table.shape[0], dtype=jnp.int32)[None, :]
    return jnp.sum(jnp.where(hits, table[None, :], jnp.float32(0.0)), axis=1)


def moves(n_occ, rule):
    pairs = []
    half = n_occ // 2
    for i in range(n_occ):
        for chip in range(2):
            for core in range(2):
                j, to = rule(i, core)
                j %= n_occ
                flip = (i // half) ^ (j // half)
                pairs.append((i * 4 + chip * 2 + core, j * 4 + (chip ^ flip) * 2 + to))
    return pairs


def swap(n_occ, mask):
    return [(i * 4 + o, i * 4 + (o ^ mask)) for i in range(n_occ) for o in range(4)]


def round1(i, core):
    if core == 0:
        return i + 1, 1
    return (i + RING, 0) if i % RING else (i, 0)


def round2(i, core):
    if core == 1:
        return i + 1, 0
    return i - i % RING + (i - 1) % RING, 1


def round3(i, core):
    return (i + 1, 1) if core == 0 else (i - 1, 0)


def round4(i, core):
    return (i + 1, 0) if core == 1 else (i - 1, 1)


def sds(shape, dtype):
    return jax.ShapeDtypeStruct(shape, dtype)


def cost(flops, nbytes):
    return pl.CostEstimate(flops=flops, bytes_accessed=nbytes, transcendentals=0)


def amp_kernel(sc, own, x, evc, evr, eo, s_out, w_out, acc, *, half, steps, slot):
    t = pl.program_id(0)
    prod = lax.dot_general(x[...], own[...], NT, preferred_element_type=F32)

    @pl.when(t == 0)
    def _():
        acc[...] = prod

    @pl.when(t > 0)
    def _():
        acc[...] += prod

    @pl.when(t == steps - 1)
    def _():
        h = sc[0]
        e = jnp.concatenate([evc[...]] * (half // 128), axis=1)

        def amp(first):
            cols = pl.ds(pl.multiple_of(first * half, half), half)
            return acc[:, cols] / (e + evr[:, cols] - eo[sc[3]] - eo[sc[4 + slot]])

        s_out[...] = amp(1 - h).astype(s_out.dtype)
        mine = amp(h)
        w_out[...] = (2.0 * mine - mine.T).astype(BF16)


def fill(w, h, group, half, s, q, v):
    def put(g, at):
        @pl.when(h == g)
        def _():
            w[:, at : at + half] = v[...]

        @pl.when(h != g)
        def _():
            w[:, at : at + half] = (2.0 * s[...].astype(F32) - q[...].astype(F32).T).astype(BF16)

    for at, g in enumerate(group):
        put(g, at * half)


def gamma_kernel(sc, *refs, n, half, early):
    xs, mixes, refs = refs[:n], refs[n : 4 * n], refs[4 * n :]
    before = refs[:2] if early else None
    outs, ws = refs[2 if early else 0 :][:2], refs[4 if early else 2 :]

    @pl.when(pl.program_id(0) == 0)
    def _():
        for k in range(n):
            fill(ws[k], sc[0], (0, 1), half, *mixes[3 * k : 3 * k + 3])

    res = lax.dot_general(xs[0][...], ws[0][...], TN, preferred_element_type=F32)
    for k in range(1, n):
        res += lax.dot_general(xs[k][...], ws[k][...], TN, preferred_element_type=F32)
    for g in range(2):
        term = res[:, g * half : (g + 1) * half]
        outs[g][...] = term + before[g][...] if early else term


def last_kernel(sc, x, s, q, v, early, keep, send, w, *, half, group):
    @pl.when(pl.program_id(0) == 0)
    def _():
        fill(w, sc[0], (group,), half, s, q, v)

    res = early[...] + lax.dot_general(x[...], w[...], TN, preferred_element_type=F32)
    res = res.reshape(res.shape[0] // 32, 2, 2, 8, res.shape[1])
    a, b = res[:, :, 0], res[:, :, 1]
    first = sc[1] == 0
    keep[...] = jnp.where(first, a, b)
    send[...] = jnp.where(first, b, a)


def body(
    factors, occ_level, vir_level, occupied_energy_levels, vir_table, virtual_coefficient_matrix
):
    n_occ = lax.axis_size("occ")
    occ_index = lax.axis_index("occ")
    off_index = lax.axis_index("off")
    chip = off_index // 2
    core = off_index % 2
    own = factors[0]
    n_vir, n_aux = own.shape
    half = n_vir // 2
    h = chip ^ (occ_index // (n_occ // 2))
    partners = [(occ_index - jnp.where(core == 0, a, b)) % n_occ for a, b in ((0, 1), (2, 7), (6, 3), (4, 5))]
    sc = jnp.stack([h, core, chip, occ_index, *partners]).astype(jnp.int32)

    x0 = lax.dynamic_slice_in_dim(own, h * half, half, 0)
    x1 = lax.ppermute(x0, BOTH, moves(n_occ, round1))
    x2 = lax.ppermute(x1, BOTH, moves(n_occ, round2))

    ev = lookup(vir_level, vir_table)
    eo = lookup(occ_level, occupied_energy_levels)
    evr = ev[None, :]
    evc = jnp.broadcast_to(lax.dynamic_slice_in_dim(ev, h * half, half, 0)[:, None], (half, 128))

    steps = 2
    tile = n_aux // steps

    def amp(x, slot, s_dtype):
        return pl.pallas_call(
            functools.partial(amp_kernel, half=half, steps=steps, slot=slot),
            out_shape=(sds((half, half), s_dtype), sds((half, half), BF16)),
            grid_spec=pltpu.PrefetchScalarGridSpec(
                num_scalar_prefetch=1,
                grid=(steps,),
                in_specs=[
                    pl.BlockSpec((n_vir, tile), lambda t, s: (0, t)),
                    pl.BlockSpec((half, tile), lambda t, s: (0, t)),
                    pl.BlockSpec((half, 128), lambda t, s: (0, 0)),
                    pl.BlockSpec((1, n_vir), lambda t, s: (0, 0)),
                    pl.BlockSpec(memory_space=pltpu.SMEM),
                ],
                out_specs=[pl.BlockSpec((half, half), lambda t, s: (0, 0))] * 2,
                scratch_shapes=[pltpu.VMEM((half, n_vir), F32)],
            ),
            cost_estimate=cost(2 * n_vir * half * n_aux, 2 * n_aux * (n_vir + half)),
            name="amp",
        )(sc, own, x, evc, evr, eo)

    def exchange(s):
        return lax.ppermute(s, BOTH, swap(n_occ, 2))

    def ring(x, rule):
        return lax.ppermute(x, BOTH, moves(n_occ, rule))

    tiles = 4
    tile_p = n_aux // tiles
    whole = pl.BlockSpec((half, half), lambda t, s: (0, 0))
    x_spec = pl.BlockSpec((half, tile_p), lambda t, s: (0, t))
    row_spec = pl.BlockSpec((tile_p, half), lambda t, s: (t, 0))

    def gamma(xs, mixes, early=None):
        n = len(xs)
        return pl.pallas_call(
            functools.partial(gamma_kernel, n=n, half=half, early=early is not None),
            out_shape=(sds((n_aux, half), F32),) * 2,
            grid_spec=pltpu.PrefetchScalarGridSpec(
                num_scalar_prefetch=1,
                grid=(tiles,),
                in_specs=[x_spec] * n + [whole] * (3 * n) + ([] if early is None else [row_spec] * 2),
                out_specs=[row_spec] * 2,
                scratch_shapes=[pltpu.VMEM((half, n_vir), BF16)] * n,
            ),
            cost_estimate=cost(2 * n * n_aux * half * n_vir, 2 * n * n_aux * half + 4 * n_aux * n_vir),
            name="gamma",
        )(sc, *xs, *(m for mix in mixes for m in mix), *(early or ()))

    y1 = jnp.where(core == 0, x0, x1)
    s1, v1 = amp(y1, 0, F32)
    q1 = exchange(s1)
    x2, _ = lax.optimization_barrier((x2, s1))
    x3 = ring(x2, round3)
    s2, v2 = amp(x2, 1, F32)
    q2 = exchange(s2)
    x3, _ = lax.optimization_barrier((x3, s2))
    x4 = ring(x3, round4)
    s3, v3 = amp(x3, 2, F32)
    q3 = exchange(s3)
    early = gamma([y1, x2], [(s1, q1, v1), (s2, q2, v2)])
    x4, _, early = lax.optimization_barrier((x4, s3, early))
    s4, v4 = amp(x4, 3, BF16)
    q4 = exchange(s4)
    v3, _ = lax.optimization_barrier((v3, s4))
    early = gamma([x3], [(s3, q3, v3)], early)

    groups = tile_p // 32

    def last(g, early):
        return pl.pallas_call(
            functools.partial(last_kernel, half=half, group=g),
            out_shape=(sds((n_occ, 2, 8, half), F32),) * 2,
            grid_spec=pltpu.PrefetchScalarGridSpec(
                num_scalar_prefetch=1,
                grid=(tiles,),
                in_specs=[x_spec] + [whole] * 3 + [row_spec],
                out_specs=[pl.BlockSpec((groups, 2, 8, half), lambda t, s: (t, 0, 0, 0))] * 2,
                scratch_shapes=[pltpu.VMEM((half, half), BF16)],
            ),
            cost_estimate=cost(n_aux * half * n_vir, 2 * n_aux * (n_vir + half)),
            name="last",
        )(sc, x4, s4, q4, v4, early)

    def part(keep, got, c):
        a = lax.dynamic_index_in_dim(keep, c, 1, keepdims=False)
        return a + lax.dynamic_index_in_dim(got, c, 1, keepdims=False)

    def finish(g, keep, got, far):
        low = (part(keep, got, chip) + far.astype(F32)).astype(BF16)
        mine = lax.all_to_all(low, "occ", split_axis=0, concat_axis=0, tiled=True)
        c = virtual_coefficient_matrix[g * half : (g + 1) * half]
        return jnp.einsum("sbd,dw->sbw", mine, c, preferred_element_type=F32)

    keep0, send0 = last(0, early[0])
    early1, send0 = lax.optimization_barrier((early[1], send0))
    got0 = lax.ppermute(send0, BOTH, swap(n_occ, 1))
    keep1, send1 = last(1, early1)
    away0 = part(keep0, got0, 1 - chip).astype(BF16)
    away0, send1 = lax.optimization_barrier((away0, send1))
    far0 = lax.ppermute(away0, BOTH, swap(n_occ, 2))
    got1 = lax.ppermute(send1, BOTH, swap(n_occ, 1))
    away1 = part(keep1, got1, 1 - chip)
    away1, far0 = lax.optimization_barrier((away1, far0))
    far1 = lax.ppermute(away1, BOTH, swap(n_occ, 2))
    return finish(0, keep0, got0, far0) + finish(1, keep1, got1, far1)


def solution(mesh):
    in_specs = (P("occ", None, None), P(), P(), P(), P(), P())
    out_specs = P(None, ("occ", "off"), None)
    return jax.shard_map(body, mesh=mesh, in_specs=in_specs, out_specs=out_specs, check_vma=False)
```

```python
import functools

import jax
import jax.numpy as jnp
from jax import lax
from jax.experimental import pallas as pl
from jax.experimental.pallas import tpu as pltpu
from jax.sharding import PartitionSpec as P


BOTH = ("occ", "off")
F32 = jnp.float32
BF16 = jnp.bfloat16
RING = 8
TN = (((0,), (0,)), ((), ()))
NT = (((1,), (1,)), ((), ()))


def lookup(level, table):
    hits = level[:, None] == jnp.arange(table.shape[0], dtype=jnp.int32)[None, :]
    return jnp.sum(jnp.where(hits, table[None, :], jnp.float32(0.0)), axis=1)


def moves(n_occ, rule):
    pairs = []
    half = n_occ // 2
    for i in range(n_occ):
        for chip in range(2):
            for core in range(2):
                j, to = rule(i, core)
                j %= n_occ
                flip = (i // half) ^ (j // half)
                pairs.append((i * 4 + chip * 2 + core, j * 4 + (chip ^ flip) * 2 + to))
    return pairs


def swap(n_occ, mask):
    return [(i * 4 + o, i * 4 + (o ^ mask)) for i in range(n_occ) for o in range(4)]


def round1(i, core):
    if core == 0:
        return i + 1, 1
    return (i + RING, 0) if i % RING else (i, 0)


def round2(i, core):
    if core == 1:
        return i + 1, 0
    return i - i % RING + (i - 1) % RING, 1


def round3(i, core):
    return (i + 1, 1) if core == 0 else (i - 1, 0)


def round4(i, core):
    return (i + 1, 0) if core == 1 else (i - 1, 1)


def sds(shape, dtype):
    return jax.ShapeDtypeStruct(shape, dtype)


def cost(flops, nbytes):
    return pl.CostEstimate(flops=flops, bytes_accessed=nbytes, transcendentals=0)


def amp_kernel(sc, own, xa, xb, evc, evr, eo, s_out, w_out, acc, *, half, slot):
    t = pl.program_id(0)

    @pl.when(t == 0)
    def _():
        acc[...] = lax.dot_general(xa[...], own[...], NT, preferred_element_type=F32)

    @pl.when(t == 1)
    def _():
        h = sc[0]
        acc[...] += lax.dot_general(xb[...], own[...], NT, preferred_element_type=F32)
        e = jnp.concatenate([evc[...]] * (half // 128), axis=1)

        def amp(first):
            cols = pl.ds(pl.multiple_of(first * half, half), half)
            return acc[:, cols] / (e + evr[:, cols] - eo[sc[3]] - eo[sc[4 + slot]])

        s_out[...] = amp(1 - h).astype(s_out.dtype)
        mine = amp(h)
        w_out[...] = (2.0 * mine - mine.T).astype(BF16)


def fill(w, h, group, half, s, q, v):
    def put(g, at):
        @pl.when(h == g)
        def _():
            w[:, at : at + half] = v[...]

        @pl.when(h != g)
        def _():
            w[:, at : at + half] = (2.0 * s[...].astype(F32) - q[...].astype(F32).T).astype(BF16)

    for at, g in enumerate(group):
        put(g, at * half)


def products(xs, ws):
    first = pl.program_id(0) < pl.num_programs(0) // 2
    res = None
    for (xa, xb), w in zip(xs, ws):
        x = jnp.where(first, xa[...], xb[...])
        term = lax.dot_general(x, w[...], TN, preferred_element_type=F32)
        res = term if res is None else res + term
    return res


def gamma_kernel(sc, *refs, n, half, early):
    xs = [refs[2 * k : 2 * k + 2] for k in range(n)]
    mixes, refs = refs[2 * n : 5 * n], refs[5 * n :]
    before = refs[0] if early else None
    out, ws = refs[1 if early else 0], refs[2 if early else 1 :]

    @pl.when(pl.program_id(0) == 0)
    def _():
        for k in range(n):
            fill(ws[k], sc[0], (0, 1), half, *mixes[3 * k : 3 * k + 3])

    res = products(xs, ws)
    out[...] = res + before[...] if early else res


def last_kernel(sc, xa, xb, s, q, v, early, keep0, keep1, send0, send1, w, *, half):
    @pl.when(pl.program_id(0) == 0)
    def _():
        fill(w, sc[0], (0, 1), half, s, q, v)

    res = early[...] + products([(xa, xb)], [w])
    res = res.reshape(res.shape[0] // 32, 2, 2, 8, res.shape[1])
    a, b = res[:, :, 0], res[:, :, 1]
    first = sc[1] == 0
    keep, send = jnp.where(first, a, b), jnp.where(first, b, a)
    keep0[...] = keep[..., :half]
    keep1[...] = keep[..., half:]
    send0[...] = send[..., :half]
    send1[...] = send[..., half:]


def body(
    factors, occ_level, vir_level, occupied_energy_levels, vir_table, virtual_coefficient_matrix
):
    n_occ = lax.axis_size("occ")
    occ_index = lax.axis_index("occ")
    off_index = lax.axis_index("off")
    chip = off_index // 2
    core = off_index % 2
    own = factors[0]
    n_vir, n_aux = own.shape
    half = n_vir // 2
    h = chip ^ (occ_index // (n_occ // 2))
    partners = [(occ_index - jnp.where(core == 0, a, b)) % n_occ for a, b in ((0, 1), (2, 7), (6, 3), (4, 5))]
    sc = jnp.stack([h, core, chip, occ_index, *partners]).astype(jnp.int32)

    def ring(x, rule):
        return lax.ppermute(x, BOTH, moves(n_occ, rule))

    def exchange(s):
        return lax.ppermute(s, BOTH, swap(n_occ, 2))

    tile = n_aux // 2
    x0 = [lax.dynamic_slice(own, (h * half, p * tile), (half, tile)) for p in range(2)]
    x1 = [ring(x0[p], round1) for p in range(2)]
    x2 = [ring(x1[p], round2) for p in range(2)]

    ev = lookup(vir_level, vir_table)
    eo = lookup(occ_level, occupied_energy_levels)
    evr = ev[None, :]
    evc = jnp.broadcast_to(lax.dynamic_slice_in_dim(ev, h * half, half, 0)[:, None], (half, 128))

    def amp(x, slot, s_dtype):
        return pl.pallas_call(
            functools.partial(amp_kernel, half=half, slot=slot),
            out_shape=(sds((half, half), s_dtype), sds((half, half), BF16)),
            grid_spec=pltpu.PrefetchScalarGridSpec(
                num_scalar_prefetch=1,
                grid=(2,),
                in_specs=[
                    pl.BlockSpec((n_vir, tile), lambda t, s: (0, t)),
                    pl.BlockSpec((half, tile), lambda t, s: (0, 0)),
                    pl.BlockSpec((half, tile), lambda t, s: (0, 0)),
                    pl.BlockSpec((half, 128), lambda t, s: (0, 0)),
                    pl.BlockSpec((1, n_vir), lambda t, s: (0, 0)),
                    pl.BlockSpec(memory_space=pltpu.SMEM),
                ],
                out_specs=[pl.BlockSpec((half, half), lambda t, s: (0, 0))] * 2,
                scratch_shapes=[pltpu.VMEM((half, n_vir), F32)],
            ),
            cost_estimate=cost(2 * n_vir * half * n_aux, 2 * n_aux * (n_vir + half)),
            name="amp",
        )(sc, own, *x, evc, evr, eo)

    tiles = 4
    tile_p = n_aux // tiles
    whole = pl.BlockSpec((half, half), lambda t, s: (0, 0))
    x_specs = [
        pl.BlockSpec((half, tile_p), lambda t, s: (0, jnp.minimum(t, 1))),
        pl.BlockSpec((half, tile_p), lambda t, s: (0, jnp.maximum(t - 2, 0))),
    ]
    row_spec = pl.BlockSpec((tile_p, n_vir), lambda t, s: (t, 0))

    def gamma(xs, mixes, early=()):
        n = len(xs)
        return pl.pallas_call(
            functools.partial(gamma_kernel, n=n, half=half, early=len(early) > 0),
            out_shape=sds((n_aux, n_vir), F32),
            grid_spec=pltpu.PrefetchScalarGridSpec(
                num_scalar_prefetch=1,
                grid=(tiles,),
                in_specs=x_specs * n + [whole] * (3 * n) + [row_spec] * len(early),
                out_specs=row_spec,
                scratch_shapes=[pltpu.VMEM((half, n_vir), BF16)] * n,
            ),
            cost_estimate=cost(2 * n * n_aux * half * n_vir, 2 * n * n_aux * half + 4 * n_aux * n_vir),
            name="gamma",
        )(sc, *(a for x in xs for a in x), *(m for mix in mixes for m in mix), *early)

    y1 = [jnp.where(core == 0, x0[p], x1[p]) for p in range(2)]
    s1, v1 = amp(y1, 0, F32)
    q1 = exchange(s1)
    x3 = [ring(x2[p], round3) for p in range(2)]
    s2, v2 = amp(x2, 1, F32)
    q2 = exchange(s2)
    x4 = [ring(x3[p], round4) for p in range(2)]
    s3, v3 = amp(x3, 2, F32)
    q3 = exchange(s3)
    early = gamma([y1, x2], [(s1, q1, v1), (s2, q2, v2)])
    x4[0], _ = lax.optimization_barrier((x4[0], s3))
    x4[1], early = lax.optimization_barrier((x4[1], early))
    s4, v4 = amp(x4, 3, BF16)
    q4 = exchange(s4)
    v3, _ = lax.optimization_barrier((v3, s4))
    early = gamma([x3], [(s3, q3, v3)], (early,))

    groups = tile_p // 32
    keep0, keep1, send0, send1 = pl.pallas_call(
        functools.partial(last_kernel, half=half),
        out_shape=(sds((n_occ, 2, 8, half), F32),) * 4,
        grid_spec=pltpu.PrefetchScalarGridSpec(
            num_scalar_prefetch=1,
            grid=(tiles,),
            in_specs=x_specs + [whole] * 3 + [row_spec],
            out_specs=[pl.BlockSpec((groups, 2, 8, half), lambda t, s: (t, 0, 0, 0))] * 4,
            scratch_shapes=[pltpu.VMEM((half, n_vir), BF16)],
        ),
        cost_estimate=cost(2 * n_aux * half * n_vir, 2 * n_aux * (4 * n_vir + half)),
        name="last",
    )(sc, *x4, s4, q4, v4, early)

    def part(keep, got, c):
        a = lax.dynamic_index_in_dim(keep, c, 1, keepdims=False)
        return a + lax.dynamic_index_in_dim(got, c, 1, keepdims=False)

    def low(keep, got, far):
        return (part(keep, got, chip) + far.astype(F32)).astype(BF16)

    def finish(g, low):
        mine = lax.all_to_all(low, "occ", split_axis=0, concat_axis=0, tiled=True)
        c = virtual_coefficient_matrix[g * half : (g + 1) * half]
        return jnp.einsum("sbd,dw->sbw", mine, c, preferred_element_type=F32)

    got0 = lax.ppermute(send0, BOTH, swap(n_occ, 1))
    away0 = part(keep0, got0, 1 - chip).astype(BF16)
    far0 = lax.ppermute(away0, BOTH, swap(n_occ, 2))
    got1 = lax.ppermute(send1, BOTH, swap(n_occ, 1))
    away1 = part(keep1, got1, 1 - chip)
    away1, _ = lax.optimization_barrier((away1, far0))
    far1 = lax.ppermute(away1, BOTH, swap(n_occ, 2))
    return finish(1, low(keep1, got1, far1)) + finish(0, low(keep0, got0, far0))


def solution(mesh):
    in_specs = (P("occ", None, None), P(), P(), P(), P(), P())
    out_specs = P(None, ("occ", "off"), None)
    return jax.shard_map(body, mesh=mesh, in_specs=in_specs, out_specs=out_specs, check_vma=False)
```

```python
import functools

import jax
import jax.numpy as jnp
from jax import lax
from jax.experimental import pallas as pl
from jax.experimental.pallas import tpu as pltpu
from jax.sharding import PartitionSpec as P


BOTH = ("occ", "off")
F32 = jnp.float32
BF16 = jnp.bfloat16
RING = 8
TN = (((0,), (0,)), ((), ()))
NT = (((1,), (1,)), ((), ()))


def lookup(level, table):
    hits = level[:, None] == jnp.arange(table.shape[0], dtype=jnp.int32)[None, :]
    return jnp.sum(jnp.where(hits, table[None, :], jnp.float32(0.0)), axis=1)


def moves(n_occ, rule):
    pairs = []
    half = n_occ // 2
    for i in range(n_occ):
        for chip in range(2):
            for core in range(2):
                j, to = rule(i, core)
                j %= n_occ
                flip = (i // half) ^ (j // half)
                pairs.append((i * 4 + chip * 2 + core, j * 4 + (chip ^ flip) * 2 + to))
    return pairs


def swap(n_occ, mask):
    return [(i * 4 + o, i * 4 + (o ^ mask)) for i in range(n_occ) for o in range(4)]


def up(i, core):
    return i + 1, core


def down(i, core):
    return i - 1, core


def over(i, core):
    return (i + RING, core) if i % RING else (i, core)


def row_down(i, core):
    return i - i % RING + (i - 1) % RING, core


def last_a(i, core):
    return (i + 1, 0) if core == 0 else (i - 1, 1)


def last_b(i, core):
    return (i - 1, 1) if core == 0 else (i + 1, 0)


def sds(shape, dtype):
    return jax.ShapeDtypeStruct(shape, dtype)


def cost(flops, nbytes):
    return pl.CostEstimate(flops=flops, bytes_accessed=nbytes, transcendentals=0)


def amp_kernel(sc, own, xa, xb, evc, evr, eo, s_out, w_out, acc, *, half, slot):
    t = pl.program_id(0)

    @pl.when(t == 0)
    def _():
        acc[...] = lax.dot_general(xa[...], own[...], NT, preferred_element_type=F32)

    @pl.when(t == 1)
    def _():
        h = sc[0]
        acc[...] += lax.dot_general(xb[...], own[...], NT, preferred_element_type=F32)
        e = jnp.concatenate([evc[...]] * (half // 128), axis=1)

        def amp(first):
            cols = pl.ds(pl.multiple_of(first * half, half), half)
            return acc[:, cols] / (e + evr[:, cols] - eo[sc[3]] - eo[sc[4 + slot]])

        s_out[...] = amp(1 - h).astype(s_out.dtype)
        mine = amp(h)
        w_out[...] = (2.0 * mine - mine.T).astype(BF16)


def fill(w, h, group, half, s, q, v):
    def put(g, at):
        @pl.when(h == g)
        def _():
            w[:, at : at + half] = v[...]

        @pl.when(h != g)
        def _():
            w[:, at : at + half] = (2.0 * s[...].astype(F32) - q[...].astype(F32).T).astype(BF16)

    for at, g in enumerate(group):
        put(g, at * half)


def products(xs, ws):
    first = pl.program_id(0) < pl.num_programs(0) // 2
    res = None
    for (xa, xb), w in zip(xs, ws):
        x = jnp.where(first, xa[...], xb[...])
        term = lax.dot_general(x, w[...], TN, preferred_element_type=F32)
        res = term if res is None else res + term
    return res


def gamma_kernel(sc, *refs, n, half, early):
    xs = [refs[2 * k : 2 * k + 2] for k in range(n)]
    mixes, refs = refs[2 * n : 5 * n], refs[5 * n :]
    before = refs[0] if early else None
    out, ws = refs[1 if early else 0], refs[2 if early else 1 :]

    @pl.when(pl.program_id(0) == 0)
    def _():
        for k in range(n):
            fill(ws[k], sc[0], (0, 1), half, *mixes[3 * k : 3 * k + 3])

    res = products(xs, ws)
    out[...] = res + before[...] if early else res


def last_kernel(sc, xa, xb, s, q, v, early, keep0, keep1, send0, send1, w, *, half):
    @pl.when(pl.program_id(0) == 0)
    def _():
        fill(w, sc[0], (0, 1), half, s, q, v)

    res = early[...] + products([(xa, xb)], [w])
    res = res.reshape(res.shape[0] // 32, 2, 2, 8, res.shape[1])
    a, b = res[:, :, 0], res[:, :, 1]
    first = sc[1] == 0
    keep, send = jnp.where(first, a, b), jnp.where(first, b, a)
    keep0[...] = keep[..., :half]
    keep1[...] = keep[..., half:]
    send0[...] = send[..., :half]
    send1[...] = send[..., half:]


def body(
    factors, occ_level, vir_level, occupied_energy_levels, vir_table, virtual_coefficient_matrix
):
    n_occ = lax.axis_size("occ")
    occ_index = lax.axis_index("occ")
    off_index = lax.axis_index("off")
    chip = off_index // 2
    core = off_index % 2
    own = factors[0]
    n_vir, n_aux = own.shape
    half = n_vir // 2
    h = chip ^ (occ_index // (n_occ // 2))
    partners = [(occ_index - jnp.where(core == 0, a, b)) % n_occ for a, b in ((1, 0), (2, 7), (3, 6), (4, 5))]
    sc = jnp.stack([h, core, chip, occ_index, *partners]).astype(jnp.int32)

    def send(x, pairs):
        return lax.ppermute(x, BOTH, pairs)

    def exchange(s):
        return send(s, swap(n_occ, 2))

    def other_core(x):
        return send(x, swap(n_occ, 1))

    def choose(a, b):
        return jnp.where(core == 0, a, b)

    tile = n_aux // 2
    x0m, x0o = [lax.dynamic_slice(own, (h * half, c * tile), (half, tile)) for c in (core, 1 - core)]
    p1 = send(x0m, moves(n_occ, up))
    m1 = send(x0m, moves(n_occ, over))
    p2 = send(p1, moves(n_occ, up))
    m2 = send(m1, moves(n_occ, row_down))
    p3 = send(p2, moves(n_occ, up))
    m3 = send(m2, moves(n_occ, down))
    a3, b3 = choose(p3, m3), choose(m3, p3)
    x1 = [choose(p1, x0m), choose(other_core(p1), x0o)]
    x2 = [choose(p2, m2), other_core(choose(m2, p2))]
    x3 = [a3, other_core(b3)]
    x4 = [send(a3, moves(n_occ, last_a)), send(b3, moves(n_occ, last_b))]

    ev = lookup(vir_level, vir_table)
    eo = lookup(occ_level, occupied_energy_levels)
    evr = ev[None, :]
    evc = jnp.broadcast_to(lax.dynamic_slice_in_dim(ev, h * half, half, 0)[:, None], (half, 128))

    def amp(x, slot, s_dtype):
        return pl.pallas_call(
            functools.partial(amp_kernel, half=half, slot=slot),
            out_shape=(sds((half, half), s_dtype), sds((half, half), BF16)),
            grid_spec=pltpu.PrefetchScalarGridSpec(
                num_scalar_prefetch=1,
                grid=(2,),
                in_specs=[
                    pl.BlockSpec((n_vir, tile), lambda t, s: (0, (t + s[1]) % 2)),
                    pl.BlockSpec((half, tile), lambda t, s: (0, 0)),
                    pl.BlockSpec((half, tile), lambda t, s: (0, 0)),
                    pl.BlockSpec((half, 128), lambda t, s: (0, 0)),
                    pl.BlockSpec((1, n_vir), lambda t, s: (0, 0)),
                    pl.BlockSpec(memory_space=pltpu.SMEM),
                ],
                out_specs=[pl.BlockSpec((half, half), lambda t, s: (0, 0))] * 2,
                scratch_shapes=[pltpu.VMEM((half, n_vir), F32)],
            ),
            cost_estimate=cost(2 * n_vir * half * n_aux, 2 * n_aux * (n_vir + half)),
            name="amp",
        )(sc, own, *x, evc, evr, eo)

    tiles = 4
    tile_p = n_aux // tiles
    whole = pl.BlockSpec((half, half), lambda t, s: (0, 0))
    x_specs = [
        pl.BlockSpec((half, tile_p), lambda t, s: (0, jnp.minimum(t, 1))),
        pl.BlockSpec((half, tile_p), lambda t, s: (0, jnp.maximum(t - 2, 0))),
    ]
    where_p = lambda t, s: (t + 2 * s[1]) % tiles
    row_spec = pl.BlockSpec((tile_p, n_vir), lambda t, s: (where_p(t, s), 0))

    def gamma(xs, mixes, early=()):
        n = len(xs)
        return pl.pallas_call(
            functools.partial(gamma_kernel, n=n, half=half, early=len(early) > 0),
            out_shape=sds((n_aux, n_vir), F32),
            grid_spec=pltpu.PrefetchScalarGridSpec(
                num_scalar_prefetch=1,
                grid=(tiles,),
                in_specs=x_specs * n + [whole] * (3 * n) + [row_spec] * len(early),
                out_specs=row_spec,
                scratch_shapes=[pltpu.VMEM((half, n_vir), BF16)] * n,
            ),
            cost_estimate=cost(2 * n * n_aux * half * n_vir, 2 * n * n_aux * half + 4 * n_aux * n_vir),
            name="gamma",
        )(sc, *(a for x in xs for a in x), *(m for mix in mixes for m in mix), *early)

    s1, v1 = amp(x1, 0, F32)
    q1 = exchange(s1)
    s2, v2 = amp(x2, 1, F32)
    q2 = exchange(s2)
    s3, v3 = amp(x3, 2, F32)
    q3 = exchange(s3)
    early = gamma([x1, x2], [(s1, q1, v1), (s2, q2, v2)])
    s4, v4 = amp(x4, 3, BF16)
    q4 = exchange(s4)
    v3, _ = lax.optimization_barrier((v3, s4))
    early = gamma([x3], [(s3, q3, v3)], (early,))

    groups = tile_p // 32
    keep0, keep1, send0, send1 = pl.pallas_call(
        functools.partial(last_kernel, half=half),
        out_shape=(sds((n_occ, 2, 8, half), F32),) * 4,
        grid_spec=pltpu.PrefetchScalarGridSpec(
            num_scalar_prefetch=1,
            grid=(tiles,),
            in_specs=x_specs + [whole] * 3 + [row_spec],
            out_specs=[pl.BlockSpec((groups, 2, 8, half), lambda t, s: (where_p(t, s), 0, 0, 0))] * 4,
            scratch_shapes=[pltpu.VMEM((half, n_vir), BF16)],
        ),
        cost_estimate=cost(2 * n_aux * half * n_vir, 2 * n_aux * (4 * n_vir + half)),
        name="last",
    )(sc, *x4, s4, q4, v4, early)

    def part(keep, got, c):
        a = lax.dynamic_index_in_dim(keep, c, 1, keepdims=False)
        return a + lax.dynamic_index_in_dim(got, c, 1, keepdims=False)

    def low(keep, got, far):
        return (part(keep, got, chip) + far.astype(F32)).astype(BF16)

    def finish(g, low):
        mine = lax.all_to_all(low, "occ", split_axis=0, concat_axis=0, tiled=True)
        c = virtual_coefficient_matrix[g * half : (g + 1) * half]
        return jnp.einsum("sbd,dw->sbw", mine, c, preferred_element_type=F32)

    got0 = lax.ppermute(send0, BOTH, swap(n_occ, 1))
    away0 = part(keep0, got0, 1 - chip).astype(BF16)
    far0 = lax.ppermute(away0, BOTH, swap(n_occ, 2))
    got1 = lax.ppermute(send1, BOTH, swap(n_occ, 1))
    away1 = part(keep1, got1, 1 - chip)
    away1, _ = lax.optimization_barrier((away1, far0))
    far1 = lax.ppermute(away1, BOTH, swap(n_occ, 2))
    return finish(1, low(keep1, got1, far1)) + finish(0, low(keep0, got0, far0))


def solution(mesh):
    in_specs = (P("occ", None, None), P(), P(), P(), P(), P())
    out_specs = P(None, ("occ", "off"), None)
    return jax.shard_map(body, mesh=mesh, in_specs=in_specs, out_specs=out_specs, check_vma=False)
```

```python
import functools

import jax
import jax.numpy as jnp
from jax import lax
from jax.experimental import pallas as pl
from jax.experimental.pallas import tpu as pltpu
from jax.sharding import PartitionSpec as P


BOTH = ("occ", "off")
F32 = jnp.float32
BF16 = jnp.bfloat16
RING = 8
TN = (((0,), (0,)), ((), ()))
NT = (((1,), (1,)), ((), ()))


def lookup(level, table):
    hits = level[:, None] == jnp.arange(table.shape[0], dtype=jnp.int32)[None, :]
    return jnp.sum(jnp.where(hits, table[None, :], jnp.float32(0.0)), axis=1)


def moves(n_occ, rule):
    pairs = []
    half = n_occ // 2
    for i in range(n_occ):
        for chip in range(2):
            for core in range(2):
                j, to = rule(i, core)
                j %= n_occ
                flip = (i // half) ^ (j // half)
                pairs.append((i * 4 + chip * 2 + core, j * 4 + (chip ^ flip) * 2 + to))
    return pairs


def swap(n_occ, mask):
    return [(i * 4 + o, i * 4 + (o ^ mask)) for i in range(n_occ) for o in range(4)]


def round1(i, core):
    if core == 0:
        return i + 1, 1
    return (i + RING, 0) if i % RING else (i, 0)


def round2(i, core):
    if core == 1:
        return i + 1, 0
    return i - i % RING + (i - 1) % RING, 1


def round3(i, core):
    return (i + 1, 1) if core == 0 else (i - 1, 0)


def round4(i, core):
    return (i + 1, 0) if core == 1 else (i - 1, 1)


def sds(shape, dtype):
    return jax.ShapeDtypeStruct(shape, dtype)


def cost(flops, nbytes):
    return pl.CostEstimate(flops=flops, bytes_accessed=nbytes, transcendentals=0)


def amp_kernel(sc, own, xa, xb, evc, evr, eo, s_out, w_out, acc, *, half, slot):
    t = pl.program_id(0)

    @pl.when(t == 0)
    def _():
        acc[...] = lax.dot_general(xa[...], own[...], NT, preferred_element_type=F32)

    @pl.when(t == 1)
    def _():
        h = sc[0]
        acc[...] += lax.dot_general(xb[...], own[...], NT, preferred_element_type=F32)
        e = jnp.concatenate([evc[...]] * (half // 128), axis=1)

        def amp(first):
            cols = pl.ds(pl.multiple_of(first * half, half), half)
            return acc[:, cols] / (e + evr[:, cols] - eo[sc[3]] - eo[sc[4 + slot]])

        s_out[...] = amp(1 - h).astype(s_out.dtype)
        mine = amp(h)
        w_out[...] = (2.0 * mine - mine.T).astype(BF16)


def fill(w, s, q):
    w[...] = (2.0 * s[...].astype(F32) - q[...].astype(F32).T).astype(BF16)


def products(xs, ws):
    first = pl.program_id(0) < pl.num_programs(0) // 2
    res = None
    for (xa, xb), w in zip(xs, ws):
        x = jnp.where(first, xa[...], xb[...])
        term = lax.dot_general(x, w[...], TN, preferred_element_type=F32)
        res = term if res is None else res + term
    return res


def gamma_kernel(sc, *refs, n, half):
    xs = [refs[2 * k : 2 * k + 2] for k in range(n)]
    mixes, outs, ws = refs[2 * n : 5 * n], refs[5 * n : 5 * n + 2], refs[5 * n + 2 :]

    @pl.when(pl.program_id(0) == 0)
    def _():
        for k in range(n):
            s, q, v = mixes[3 * k : 3 * k + 3]
            ws[k][:, :half] = v[...]
            ws[k][:, half:] = (2.0 * s[...].astype(F32) - q[...].astype(F32).T).astype(BF16)

    res = products(xs, ws)
    outs[0][...] = res[:, :half]
    outs[1][...] = res[:, half:]


def last_kernel(sc, *refs, n, mixed):
    xs = [refs[2 * k : 2 * k + 2] for k in range(n)]
    per = 2 if mixed else 1
    mixes, refs = refs[2 * n : (2 + per) * n], refs[(2 + per) * n :]
    early, keep, send, ws = refs[0], refs[1], refs[2], refs[3:]
    if mixed:

        @pl.when(pl.program_id(0) == 0)
        def _():
            for k in range(n):
                fill(ws[k], *mixes[2 * k : 2 * k + 2])

    else:
        ws = mixes
    res = early[...] + products(xs, ws)
    res = res.reshape(res.shape[0] // 32, 2, 2, 8, res.shape[1])
    a, b = res[:, :, 0], res[:, :, 1]
    first = sc[1] == 0
    kept, sent = jnp.where(first, a, b), jnp.where(first, b, a)
    for c in range(2):
        keep[c] = kept[:, c]
        send[c] = sent[:, c]


def body(
    factors, occ_level, vir_level, occupied_energy_levels, vir_table, virtual_coefficient_matrix
):
    n_occ = lax.axis_size("occ")
    occ_index = lax.axis_index("occ")
    off_index = lax.axis_index("off")
    chip = off_index // 2
    core = off_index % 2
    own = factors[0]
    n_vir, n_aux = own.shape
    half = n_vir // 2
    h = chip ^ (occ_index // (n_occ // 2))
    partners = [(occ_index - jnp.where(core == 0, a, b)) % n_occ for a, b in ((0, 1), (2, 7), (6, 3), (4, 5))]
    sc = jnp.stack([h, core, chip, occ_index, *partners]).astype(jnp.int32)

    def ring(x, rule):
        return lax.ppermute(x, BOTH, moves(n_occ, rule))

    def exchange(s):
        return lax.ppermute(s, BOTH, swap(n_occ, 2))

    tile = n_aux // 2
    x0 = [lax.dynamic_slice(own, (h * half, p * tile), (half, tile)) for p in range(2)]
    x1 = [ring(x0[p], round1) for p in range(2)]
    x2 = [ring(x1[p], round2) for p in range(2)]

    ev = lookup(vir_level, vir_table)
    eo = lookup(occ_level, occupied_energy_levels)
    evr = ev[None, :]
    evc = jnp.broadcast_to(lax.dynamic_slice_in_dim(ev, h * half, half, 0)[:, None], (half, 128))

    def amp(x, slot, s_dtype):
        return pl.pallas_call(
            functools.partial(amp_kernel, half=half, slot=slot),
            out_shape=(sds((half, half), s_dtype), sds((half, half), BF16)),
            grid_spec=pltpu.PrefetchScalarGridSpec(
                num_scalar_prefetch=1,
                grid=(2,),
                in_specs=[
                    pl.BlockSpec((n_vir, tile), lambda t, s: (0, t)),
                    pl.BlockSpec((half, tile), lambda t, s: (0, 0)),
                    pl.BlockSpec((half, tile), lambda t, s: (0, 0)),
                    pl.BlockSpec((half, 128), lambda t, s: (0, 0)),
                    pl.BlockSpec((1, n_vir), lambda t, s: (0, 0)),
                    pl.BlockSpec(memory_space=pltpu.SMEM),
                ],
                out_specs=[pl.BlockSpec((half, half), lambda t, s: (0, 0))] * 2,
                scratch_shapes=[pltpu.VMEM((half, n_vir), F32)],
            ),
            cost_estimate=cost(2 * n_vir * half * n_aux, 2 * n_aux * (n_vir + half)),
            name="amp",
        )(sc, own, *x, evc, evr, eo)

    tiles = 4
    tile_p = n_aux // tiles
    whole = pl.BlockSpec((half, half), lambda t, s: (0, 0))
    x_specs = [
        pl.BlockSpec((half, tile_p), lambda t, s: (0, jnp.minimum(t, 1))),
        pl.BlockSpec((half, tile_p), lambda t, s: (0, jnp.maximum(t - 2, 0))),
    ]
    row_spec = pl.BlockSpec((tile_p, half), lambda t, s: (t, 0))

    def gamma(xs, mixes):
        n = len(xs)
        return pl.pallas_call(
            functools.partial(gamma_kernel, n=n, half=half),
            out_shape=(sds((n_aux, half), F32),) * 2,
            grid_spec=pltpu.PrefetchScalarGridSpec(
                num_scalar_prefetch=1,
                grid=(tiles,),
                in_specs=x_specs * n + [whole] * (3 * n),
                out_specs=[row_spec] * 2,
                scratch_shapes=[pltpu.VMEM((half, n_vir), BF16)] * n,
            ),
            cost_estimate=cost(2 * n * n_aux * half * n_vir, 2 * n * n_aux * half + 4 * n_aux * n_vir),
            name="gamma",
        )(sc, *(a for x in xs for a in x), *(m for mix in mixes for m in mix))

    y1 = [jnp.where(core == 0, x0[p], x1[p]) for p in range(2)]
    s1, v1 = amp(y1, 0, F32)
    q1 = exchange(s1)
    c_halves = virtual_coefficient_matrix.reshape(2, half, -1)
    c_own = jnp.where(chip == 0, c_halves, c_halves[::-1])
    x2[0], c_own = lax.optimization_barrier((x2[0], c_own))
    x3 = [ring(x2[p], round3) for p in range(2)]
    s2, v2 = amp(x2, 1, F32)
    q2 = exchange(s2)
    x4 = [ring(x3[p], round4) for p in range(2)]
    s3, v3 = amp(x3, 2, F32)
    q3 = exchange(s3)
    early = gamma([y1, x2], [(s1, q1, v1), (s2, q2, v2)])
    x4[0], _ = lax.optimization_barrier((x4[0], s3))
    x4[1], early = lax.optimization_barrier((x4[1], early))
    s4, v4 = amp(x4, 3, BF16)
    q4 = exchange(s4)

    groups = tile_p // 32

    def last(xs, mixes, early):
        n, mixed = len(xs), len(mixes) == 2 * len(xs)
        return pl.pallas_call(
            functools.partial(last_kernel, n=n, mixed=mixed),
            out_shape=(sds((2, n_occ, 8, half), F32),) * 2,
            grid_spec=pltpu.PrefetchScalarGridSpec(
                num_scalar_prefetch=1,
                grid=(tiles,),
                in_specs=x_specs * n + [whole] * len(mixes) + [row_spec],
                out_specs=[pl.BlockSpec((2, groups, 8, half), lambda t, s: (0, t, 0, 0))] * 2,
                scratch_shapes=[pltpu.VMEM((half, half), BF16)] * (n if mixed else 0),
            ),
            cost_estimate=cost(n * n_aux * half * n_vir, 2 * n_aux * (n_vir + n * half)),
            name="last",
        )(sc, *(a for x in xs for a in x), *mixes, early)

    def part(keep, got, c):
        a = lax.dynamic_index_in_dim(keep, c, 0, keepdims=False)
        return a + lax.dynamic_index_in_dim(got, c, 0, keepdims=False)

    def low(keep, got, far):
        return (part(keep, got, chip) + far.astype(F32)).astype(BF16)

    def finish(low, c):
        mine = lax.all_to_all(low, "occ", split_axis=0, concat_axis=0, tiled=True)
        mine = mine.reshape(2, n_occ // 2 * low.shape[1], half)
        return jnp.einsum("zsd,zdw->zsw", mine, c, preferred_element_type=F32)

    keep0, send0 = last([x3, x4], [v3, v4], early[0])
    early1, send0 = lax.optimization_barrier((early[1], send0))
    got0 = lax.ppermute(send0, BOTH, swap(n_occ, 1))
    away0 = part(keep0, got0, 1 - chip).astype(BF16)
    far0 = lax.ppermute(away0, BOTH, swap(n_occ, 2))
    keep1, send1 = last([x3, x4], [s3, q3, s4, q4], early1)
    got1 = lax.ppermute(send1, BOTH, swap(n_occ, 1))
    away1 = part(keep1, got1, 1 - chip)
    away1, _ = lax.optimization_barrier((away1, far0))
    far1 = lax.ppermute(away1, BOTH, swap(n_occ, 2))
    out = finish(low(keep0, got0, far1), c_own) + finish(low(keep1, got1, far0), c_own[::-1])
    return out.reshape(n_occ, -1, out.shape[-1])


def solution(mesh):
    in_specs = (P("occ", None, None), P(), P(), P(), P(), P())
    out_specs = P(None, ("occ", "off"), None)
    return jax.shard_map(body, mesh=mesh, in_specs=in_specs, out_specs=out_specs, check_vma=False)
```

```python
import functools

import jax
import jax.numpy as jnp
from jax import lax
from jax.experimental import pallas as pl
from jax.experimental.pallas import tpu as pltpu
from jax.sharding import PartitionSpec as P


BOTH = ("occ", "off")
F32 = jnp.float32
BF16 = jnp.bfloat16
RING = 8
TN = (((0,), (0,)), ((), ()))
NT = (((1,), (1,)), ((), ()))


def lookup(level, table):
    hits = level[:, None] == jnp.arange(table.shape[0], dtype=jnp.int32)[None, :]
    return jnp.sum(jnp.where(hits, table[None, :], jnp.float32(0.0)), axis=1)


def moves(n_occ, rule):
    pairs = []
    half = n_occ // 2
    for i in range(n_occ):
        for chip in range(2):
            for core in range(2):
                j, to = rule(i, core)
                j %= n_occ
                flip = (i // half) ^ (j // half)
                pairs.append((i * 4 + chip * 2 + core, j * 4 + (chip ^ flip) * 2 + to))
    return pairs


def swap(n_occ, mask):
    return [(i * 4 + o, i * 4 + (o ^ mask)) for i in range(n_occ) for o in range(4)]


def round1(i, core):
    if core == 0:
        return i + 1, 1
    return (i + RING, 0) if i % RING else (i, 0)


def round2(i, core):
    if core == 1:
        return i + 1, 0
    return i - i % RING + (i - 1) % RING, 1


def round3(i, core):
    return (i + 1, 1) if core == 0 else (i - 1, 0)


def round4(i, core):
    return (i + 1, 0) if core == 1 else (i - 1, 1)


def sds(shape, dtype):
    return jax.ShapeDtypeStruct(shape, dtype)


def cost(flops, nbytes):
    return pl.CostEstimate(flops=flops, bytes_accessed=nbytes, transcendentals=0)


def amp_kernel(sc, own, xa, xb, evc, evr, eo, s_out, w_out, acc, *, half, slot):
    t = pl.program_id(0)

    @pl.when(t == 0)
    def _():
        acc[...] = lax.dot_general(xa[...], own[...], NT, preferred_element_type=F32)

    @pl.when(t == 1)
    def _():
        h = sc[0]
        acc[...] += lax.dot_general(xb[...], own[...], NT, preferred_element_type=F32)
        e = jnp.concatenate([evc[...]] * (half // 128), axis=1)

        def amp(first):
            cols = pl.ds(pl.multiple_of(first * half, half), half)
            return acc[:, cols] / (e + evr[:, cols] - eo[sc[3]] - eo[sc[4 + slot]])

        s_out[...] = amp(1 - h).astype(s_out.dtype)
        mine = amp(h)
        w_out[...] = (2.0 * mine - mine.T).astype(BF16)


def joined(xs):
    first = pl.program_id(0) < pl.num_programs(0) // 2
    return jnp.concatenate([jnp.where(first, xa[...], xb[...]) for xa, xb in xs], axis=0)


def mix(s, q):
    return (2.0 * s[...].astype(F32) - q[...].astype(F32).T).astype(BF16)


def gamma_kernel(sc, *refs, n, half):
    xs = [refs[2 * k : 2 * k + 2] for k in range(n)]
    mixes, outs, w = refs[2 * n : 5 * n], refs[5 * n : 5 * n + 2], refs[5 * n + 2]

    @pl.when(pl.program_id(0) == 0)
    def _():
        for k in range(n):
            s, q, v = mixes[3 * k : 3 * k + 3]
            w[k * half : (k + 1) * half, :half] = v[...]
            w[k * half : (k + 1) * half, half:] = mix(s, q)

    res = lax.dot_general(joined(xs), w[...], TN, preferred_element_type=F32)
    outs[0][...] = res[:, :half]
    outs[1][...] = res[:, half:]


def last_kernel(sc, *refs, n, half, mixed):
    xs = [refs[2 * k : 2 * k + 2] for k in range(n)]
    per = 2 if mixed else 1
    mixes, refs = refs[2 * n : (2 + per) * n], refs[(2 + per) * n :]
    early, keep, send, w = refs

    @pl.when(pl.program_id(0) == 0)
    def _():
        for k in range(n):
            w[k * half : (k + 1) * half, :] = mix(*mixes[2 * k : 2 * k + 2]) if mixed else mixes[k][...]

    res = early[...] + lax.dot_general(joined(xs), w[...], TN, preferred_element_type=F32)
    res = res.reshape(res.shape[0] // 32, 2, 2, 8, res.shape[1])
    a, b = res[:, :, 0], res[:, :, 1]
    first = sc[1] == 0
    kept, sent = jnp.where(first, a, b), jnp.where(first, b, a)
    for c in range(2):
        keep[c] = kept[:, c]
        send[c] = sent[:, c]


def body(
    factors, occ_level, vir_level, occupied_energy_levels, vir_table, virtual_coefficient_matrix
):
    n_occ = lax.axis_size("occ")
    occ_index = lax.axis_index("occ")
    off_index = lax.axis_index("off")
    chip = off_index // 2
    core = off_index % 2
    own = factors[0]
    n_vir, n_aux = own.shape
    half = n_vir // 2
    h = chip ^ (occ_index // (n_occ // 2))
    partners = [(occ_index - jnp.where(core == 0, a, b)) % n_occ for a, b in ((0, 1), (2, 7), (6, 3), (4, 5))]
    sc = jnp.stack([h, core, chip, occ_index, *partners]).astype(jnp.int32)

    def ring(x, rule):
        return lax.ppermute(x, BOTH, moves(n_occ, rule))

    def exchange(s):
        return lax.ppermute(s, BOTH, swap(n_occ, 2))

    tile = n_aux // 2
    x0 = [lax.dynamic_slice(own, (h * half, p * tile), (half, tile)) for p in range(2)]
    x1 = [ring(x0[p], round1) for p in range(2)]
    x2 = [ring(x1[p], round2) for p in range(2)]

    ev = lookup(vir_level, vir_table)
    eo = lookup(occ_level, occupied_energy_levels)
    evr = ev[None, :]
    evc = jnp.broadcast_to(lax.dynamic_slice_in_dim(ev, h * half, half, 0)[:, None], (half, 128))

    def amp(x, slot, s_dtype):
        return pl.pallas_call(
            functools.partial(amp_kernel, half=half, slot=slot),
            out_shape=(sds((half, half), s_dtype), sds((half, half), BF16)),
            grid_spec=pltpu.PrefetchScalarGridSpec(
                num_scalar_prefetch=1,
                grid=(2,),
                in_specs=[
                    pl.BlockSpec((n_vir, tile), lambda t, s: (0, t)),
                    pl.BlockSpec((half, tile), lambda t, s: (0, 0)),
                    pl.BlockSpec((half, tile), lambda t, s: (0, 0)),
                    pl.BlockSpec((half, 128), lambda t, s: (0, 0)),
                    pl.BlockSpec((1, n_vir), lambda t, s: (0, 0)),
                    pl.BlockSpec(memory_space=pltpu.SMEM),
                ],
                out_specs=[pl.BlockSpec((half, half), lambda t, s: (0, 0))] * 2,
                scratch_shapes=[pltpu.VMEM((half, n_vir), F32)],
            ),
            cost_estimate=cost(2 * n_vir * half * n_aux, 2 * n_aux * (n_vir + half)),
            name="amp",
        )(sc, own, *x, evc, evr, eo)

    tiles = 2
    tile_p = n_aux // tiles
    whole = pl.BlockSpec((half, half), lambda t, s: (0, 0))
    x_specs = [
        pl.BlockSpec((half, tile_p), lambda t, s: (0, jnp.minimum(t, tiles // 2 - 1))),
        pl.BlockSpec((half, tile_p), lambda t, s: (0, jnp.maximum(t - tiles // 2, 0))),
    ]
    row_spec = pl.BlockSpec((tile_p, half), lambda t, s: (t, 0))

    def gamma(xs, mixes):
        n = len(xs)
        return pl.pallas_call(
            functools.partial(gamma_kernel, n=n, half=half),
            out_shape=(sds((n_aux, half), F32),) * 2,
            grid_spec=pltpu.PrefetchScalarGridSpec(
                num_scalar_prefetch=1,
                grid=(tiles,),
                in_specs=x_specs * n + [whole] * (3 * n),
                out_specs=[row_spec] * 2,
                scratch_shapes=[pltpu.VMEM((n * half, n_vir), BF16)],
            ),
            cost_estimate=cost(2 * n * n_aux * half * n_vir, 2 * n * n_aux * half + 4 * n_aux * n_vir),
            name="gamma",
        )(sc, *(a for x in xs for a in x), *(m for mix in mixes for m in mix))

    y1 = [jnp.where(core == 0, x0[p], x1[p]) for p in range(2)]
    s1, v1 = amp(y1, 0, F32)
    q1 = exchange(s1)
    c_halves = virtual_coefficient_matrix.reshape(2, half, -1)
    c_own = jnp.where(chip == 0, c_halves, c_halves[::-1])
    x2[0], c_own = lax.optimization_barrier((x2[0], c_own))
    x3 = [ring(x2[p], round3) for p in range(2)]
    s2, v2 = amp(x2, 1, F32)
    q2 = exchange(s2)
    x4 = [ring(x3[p], round4) for p in range(2)]
    s3, v3 = amp(x3, 2, F32)
    q3 = exchange(s3)
    early = gamma([y1, x2], [(s1, q1, v1), (s2, q2, v2)])
    x4[0], _ = lax.optimization_barrier((x4[0], s3))
    x4[1], early = lax.optimization_barrier((x4[1], early))
    s4, v4 = amp(x4, 3, BF16)
    q4 = exchange(s4)

    groups = tile_p // 32

    def last(xs, mixes, early):
        n, mixed = len(xs), len(mixes) == 2 * len(xs)
        return pl.pallas_call(
            functools.partial(last_kernel, n=n, half=half, mixed=mixed),
            out_shape=(sds((2, n_occ, 8, half), F32),) * 2,
            grid_spec=pltpu.PrefetchScalarGridSpec(
                num_scalar_prefetch=1,
                grid=(tiles,),
                in_specs=x_specs * n + [whole] * len(mixes) + [row_spec],
                out_specs=[pl.BlockSpec((2, groups, 8, half), lambda t, s: (0, t, 0, 0))] * 2,
                scratch_shapes=[pltpu.VMEM((n * half, half), BF16)],
            ),
            cost_estimate=cost(n * n_aux * half * n_vir, 2 * n_aux * (n_vir + n * half)),
            name="last",
        )(sc, *(a for x in xs for a in x), *mixes, early)

    def part(keep, got, c):
        a = lax.dynamic_index_in_dim(keep, c, 0, keepdims=False)
        return a + lax.dynamic_index_in_dim(got, c, 0, keepdims=False)

    def low(keep, got, far):
        return (part(keep, got, chip) + far.astype(F32)).astype(BF16)

    def finish(low, c):
        mine = lax.all_to_all(low, "occ", split_axis=0, concat_axis=0, tiled=True)
        mine = mine.reshape(2, n_occ // 2 * low.shape[1], half)
        return jnp.einsum("zsd,zdw->zsw", mine, c, preferred_element_type=F32)

    keep0, send0 = last([x3, x4], [v3, v4], early[0])
    early1, send0 = lax.optimization_barrier((early[1], send0))
    got0 = lax.ppermute(send0, BOTH, swap(n_occ, 1))
    away0 = part(keep0, got0, 1 - chip).astype(BF16)
    far0 = lax.ppermute(away0, BOTH, swap(n_occ, 2))
    keep1, send1 = last([x3, x4], [s3, q3, s4, q4], early1)
    got1 = lax.ppermute(send1, BOTH, swap(n_occ, 1))
    away1 = part(keep1, got1, 1 - chip).astype(BF16)
    far0, _ = lax.optimization_barrier((far0, away1))
    far1 = lax.ppermute(away1, BOTH, swap(n_occ, 2))
    low1 = low(keep1, got1, far0)
    out = finish(low(keep0, got0, far1), c_own) + finish(low1, c_own[::-1])
    return out.reshape(n_occ, -1, out.shape[-1])


def solution(mesh):
    in_specs = (P("occ", None, None), P(), P(), P(), P(), P())
    out_specs = P(None, ("occ", "off"), None)
    return jax.shard_map(body, mesh=mesh, in_specs=in_specs, out_specs=out_specs, check_vma=False)
```

```python
import functools

import jax
import jax.numpy as jnp
from jax import lax
from jax.experimental import pallas as pl
from jax.experimental.pallas import tpu as pltpu
from jax.sharding import PartitionSpec as P


BOTH = ("occ", "off")
F32 = jnp.float32
BF16 = jnp.bfloat16
RING = 8
TN = (((0,), (0,)), ((), ()))
NT = (((1,), (1,)), ((), ()))


def lookup(level, table):
    hits = level[:, None] == jnp.arange(table.shape[0], dtype=jnp.int32)[None, :]
    return jnp.sum(jnp.where(hits, table[None, :], jnp.float32(0.0)), axis=1)


def moves(n_occ, rule):
    pairs = []
    half = n_occ // 2
    for i in range(n_occ):
        for chip in range(2):
            for core in range(2):
                j, to = rule(i, core)
                j %= n_occ
                flip = (i // half) ^ (j // half)
                pairs.append((i * 4 + chip * 2 + core, j * 4 + (chip ^ flip) * 2 + to))
    return pairs


def swap(n_occ, mask):
    return [(i * 4 + o, i * 4 + (o ^ mask)) for i in range(n_occ) for o in range(4)]


def round1(i, core):
    if core == 0:
        return i + 1, 1
    return (i + RING, 0) if i % RING else (i, 0)


def round2(i, core):
    if core == 1:
        return i + 1, 0
    return i - i % RING + (i - 1) % RING, 1


def round3(i, core):
    return (i + 1, 1) if core == 0 else (i - 1, 0)


def round4(i, core):
    return (i + 1, 0) if core == 1 else (i - 1, 1)


def sds(shape, dtype):
    return jax.ShapeDtypeStruct(shape, dtype)


def cost(flops, nbytes):
    return pl.CostEstimate(flops=flops, bytes_accessed=nbytes, transcendentals=0)


def amp_kernel(sc, own, xa, xb, evc, evr, eo, s_out, w_out, acc, *, half, slot):
    t = pl.program_id(0)

    @pl.when(t == 0)
    def _():
        acc[...] = lax.dot_general(xa[...], own[...], NT, preferred_element_type=F32)

    @pl.when(t == 1)
    def _():
        h = sc[0]
        acc[...] += lax.dot_general(xb[...], own[...], NT, preferred_element_type=F32)
        e = jnp.concatenate([evc[...]] * (half // 128), axis=1)

        def amp(first):
            cols = pl.ds(pl.multiple_of(first * half, half), half)
            return acc[:, cols] / (e + evr[:, cols] - eo[sc[3]] - eo[sc[4 + slot]])

        s_out[...] = amp(1 - h).astype(s_out.dtype)
        mine = amp(h)
        w_out[...] = (2.0 * mine - mine.T).astype(BF16)


def joined(xs):
    first = pl.program_id(0) < pl.num_programs(0) // 2
    return jnp.concatenate([jnp.where(first, xa[...], xb[...]) for xa, xb in xs], axis=0)


def mix(s, q):
    return (2.0 * s[...].astype(F32) - q[...].astype(F32).T).astype(BF16)


def gamma_kernel(sc, *refs, n, half):
    xs = [refs[2 * k : 2 * k + 2] for k in range(n)]
    mixes, outs, w = refs[2 * n : 5 * n], refs[5 * n : 5 * n + 2], refs[5 * n + 2]

    @pl.when(pl.program_id(0) == 0)
    def _():
        for k in range(n):
            s, q, v = mixes[3 * k : 3 * k + 3]
            w[k * half : (k + 1) * half, :half] = v[...]
            w[k * half : (k + 1) * half, half:] = mix(s, q)

    res = lax.dot_general(joined(xs), w[...], TN, preferred_element_type=F32)
    outs[0][...] = res[:, :half]
    outs[1][...] = res[:, half:]


def last_kernel(sc, *refs, n, half, mixed):
    xs = [refs[2 * k : 2 * k + 2] for k in range(n)]
    per = 2 if mixed else 1
    mixes, refs = refs[2 * n : (2 + per) * n], refs[(2 + per) * n :]
    early, keep, send, w = refs

    @pl.when(pl.program_id(0) == 0)
    def _():
        for k in range(n):
            w[k * half : (k + 1) * half, :] = mix(*mixes[2 * k : 2 * k + 2]) if mixed else mixes[k][...]

    res = early[...] + lax.dot_general(joined(xs), w[...], TN, preferred_element_type=F32)
    res = res.reshape(res.shape[0] // 32, 2, 2, 8, res.shape[1])
    a, b = res[:, :, 0], res[:, :, 1]
    first = sc[1] == 0
    kept, sent = jnp.where(first, a, b), jnp.where(first, b, a)
    for c in range(2):
        keep[c] = kept[:, c]
        send[c] = sent[:, c]


def body(
    factors, occ_level, vir_level, occupied_energy_levels, vir_table, virtual_coefficient_matrix
):
    n_occ = lax.axis_size("occ")
    occ_index = lax.axis_index("occ")
    off_index = lax.axis_index("off")
    chip = off_index // 2
    core = off_index % 2
    own = factors[0]
    n_vir, n_aux = own.shape
    half = n_vir // 2
    h = chip ^ (occ_index // (n_occ // 2))
    partners = [(occ_index - jnp.where(core == 0, a, b)) % n_occ for a, b in ((0, 1), (2, 7), (6, 3), (4, 5))]
    sc = jnp.stack([h, core, chip, occ_index, *partners]).astype(jnp.int32)

    def ring(x, rule):
        return lax.ppermute(x, BOTH, moves(n_occ, rule))

    def exchange(s):
        return lax.ppermute(s, BOTH, swap(n_occ, 2))

    tile = n_aux // 2
    x0 = [lax.dynamic_slice(own, (h * half, p * tile), (half, tile)) for p in range(2)]
    x1 = [ring(x0[p], round1) for p in range(2)]
    x2 = [ring(x1[p], round2) for p in range(2)]

    ev = lookup(vir_level, vir_table)
    eo = lookup(occ_level, occupied_energy_levels)
    evr = ev[None, :]
    evc = jnp.broadcast_to(lax.dynamic_slice_in_dim(ev, h * half, half, 0)[:, None], (half, 128))

    def amp(x, slot, s_dtype):
        return pl.pallas_call(
            functools.partial(amp_kernel, half=half, slot=slot),
            out_shape=(sds((half, half), s_dtype), sds((half, half), BF16)),
            grid_spec=pltpu.PrefetchScalarGridSpec(
                num_scalar_prefetch=1,
                grid=(2,),
                in_specs=[
                    pl.BlockSpec((n_vir, tile), lambda t, s: (0, t)),
                    pl.BlockSpec((half, tile), lambda t, s: (0, 0)),
                    pl.BlockSpec((half, tile), lambda t, s: (0, 0)),
                    pl.BlockSpec((half, 128), lambda t, s: (0, 0)),
                    pl.BlockSpec((1, n_vir), lambda t, s: (0, 0)),
                    pl.BlockSpec(memory_space=pltpu.SMEM),
                ],
                out_specs=[pl.BlockSpec((half, half), lambda t, s: (0, 0))] * 2,
                scratch_shapes=[pltpu.VMEM((half, n_vir), F32)],
            ),
            cost_estimate=cost(2 * n_vir * half * n_aux, 2 * n_aux * (n_vir + half)),
            name="amp",
        )(sc, own, *x, evc, evr, eo)

    tiles = 2
    tile_p = n_aux // tiles
    whole = pl.BlockSpec((half, half), lambda t, s: (0, 0))
    x_specs = [
        pl.BlockSpec((half, tile_p), lambda t, s: (0, jnp.minimum(t, tiles // 2 - 1))),
        pl.BlockSpec((half, tile_p), lambda t, s: (0, jnp.maximum(t - tiles // 2, 0))),
    ]
    row_spec = pl.BlockSpec((tile_p, half), lambda t, s: (t, 0))

    def gamma(xs, mixes):
        n = len(xs)
        return pl.pallas_call(
            functools.partial(gamma_kernel, n=n, half=half),
            out_shape=(sds((n_aux, half), F32),) * 2,
            grid_spec=pltpu.PrefetchScalarGridSpec(
                num_scalar_prefetch=1,
                grid=(tiles,),
                in_specs=x_specs * n + [whole] * (3 * n),
                out_specs=[row_spec] * 2,
                scratch_shapes=[pltpu.VMEM((n * half, n_vir), BF16)],
            ),
            cost_estimate=cost(2 * n * n_aux * half * n_vir, 2 * n * n_aux * half + 4 * n_aux * n_vir),
            name="gamma",
        )(sc, *(a for x in xs for a in x), *(m for mix in mixes for m in mix))

    y1 = [jnp.where(core == 0, x0[p], x1[p]) for p in range(2)]
    s1, v1 = amp(y1, 0, F32)
    q1 = exchange(s1)
    c_halves = virtual_coefficient_matrix.reshape(2, half, -1)
    c_flip = c_halves[::-1]
    c_both = [jnp.concatenate([c[0], c[1]], axis=0) for c in (c_halves, c_flip)]
    c_own = jnp.where(chip == 0, jnp.stack(c_both), jnp.stack(c_both[::-1]))
    x2[0], c_own = lax.optimization_barrier((x2[0], c_own))
    x3 = [ring(x2[p], round3) for p in range(2)]
    s2, v2 = amp(x2, 1, F32)
    q2 = exchange(s2)
    x4 = [ring(x3[p], round4) for p in range(2)]
    s3, v3 = amp(x3, 2, F32)
    q3 = exchange(s3)
    early = gamma([y1, x2], [(s1, q1, v1), (s2, q2, v2)])
    x4[0], _ = lax.optimization_barrier((x4[0], s3))
    x4[1], early = lax.optimization_barrier((x4[1], early))
    s4, v4 = amp(x4, 3, BF16)
    q4 = exchange(s4)

    groups = tile_p // 32

    def last(xs, mixes, early):
        n, mixed = len(xs), len(mixes) == 2 * len(xs)
        return pl.pallas_call(
            functools.partial(last_kernel, n=n, half=half, mixed=mixed),
            out_shape=(sds((2, n_occ, 8, half), F32),) * 2,
            grid_spec=pltpu.PrefetchScalarGridSpec(
                num_scalar_prefetch=1,
                grid=(tiles,),
                in_specs=x_specs * n + [whole] * len(mixes) + [row_spec],
                out_specs=[pl.BlockSpec((2, groups, 8, half), lambda t, s: (0, t, 0, 0))] * 2,
                scratch_shapes=[pltpu.VMEM((n * half, half), BF16)],
            ),
            cost_estimate=cost(n * n_aux * half * n_vir, 2 * n_aux * (n_vir + n * half)),
            name="last",
        )(sc, *(a for x in xs for a in x), *mixes, early)

    def part(keep, got, c):
        a = lax.dynamic_index_in_dim(keep, c, 0, keepdims=False)
        return a + lax.dynamic_index_in_dim(got, c, 0, keepdims=False)

    def low(keep, got, far):
        return (part(keep, got, chip) + far.astype(F32)).astype(BF16)

    keep0, send0 = last([x3, x4], [v3, v4], early[0])
    early1, send0 = lax.optimization_barrier((early[1], send0))
    got0 = lax.ppermute(send0, BOTH, swap(n_occ, 1))
    away0 = part(keep0, got0, 1 - chip).astype(BF16)
    far0 = lax.ppermute(away0, BOTH, swap(n_occ, 2))
    keep1, send1 = last([x3, x4], [s3, q3, s4, q4], early1)
    got1 = lax.ppermute(send1, BOTH, swap(n_occ, 1))
    away1 = part(keep1, got1, 1 - chip).astype(BF16)
    far1 = lax.ppermute(away1, BOTH, swap(n_occ, 2))
    gamma_low = jnp.concatenate([low(keep0, got0, far1), low(keep1, got1, far0)], axis=2)
    mine = lax.all_to_all(gamma_low, "occ", split_axis=0, concat_axis=0, tiled=True)
    mine = mine.reshape(2, n_occ // 2 * mine.shape[1], n_vir)
    out = jnp.einsum("zsd,zdw->zsw", mine, c_own, preferred_element_type=F32)
    return out.reshape(n_occ, -1, out.shape[-1])


def solution(mesh):
    in_specs = (P("occ", None, None), P(), P(), P(), P(), P())
    out_specs = P(None, ("occ", "off"), None)
    return jax.shard_map(body, mesh=mesh, in_specs=in_specs, out_specs=out_specs, check_vma=False)
```

```python
import functools

import jax
import jax.numpy as jnp
from jax import lax
from jax.experimental import pallas as pl
from jax.experimental.pallas import tpu as pltpu
from jax.sharding import PartitionSpec as P


BOTH = ("occ", "off")
F32 = jnp.float32
BF16 = jnp.bfloat16
RING = 8
TN = (((0,), (0,)), ((), ()))
NT = (((1,), (1,)), ((), ()))


def lookup(level, table):
    hits = level[:, None] == jnp.arange(table.shape[0], dtype=jnp.int32)[None, :]
    return jnp.sum(jnp.where(hits, table[None, :], jnp.float32(0.0)), axis=1)


def moves(n_occ, rule):
    pairs = []
    half = n_occ // 2
    for i in range(n_occ):
        for chip in range(2):
            for core in range(2):
                j, to = rule(i, core)
                j %= n_occ
                flip = (i // half) ^ (j // half)
                pairs.append((i * 4 + chip * 2 + core, j * 4 + (chip ^ flip) * 2 + to))
    return pairs


def swap(n_occ, mask):
    return [(i * 4 + o, i * 4 + (o ^ mask)) for i in range(n_occ) for o in range(4)]


def round1(i, core):
    if core == 0:
        return i + 1, 1
    return (i + RING, 0) if i % RING else (i, 0)


def round2(i, core):
    if core == 1:
        return i + 1, 0
    return i - i % RING + (i - 1) % RING, 1


def round3(i, core):
    return (i + 1, 1) if core == 0 else (i - 1, 0)


def round4(i, core):
    return (i + 1, 0) if core == 1 else (i - 1, 1)


def sds(shape, dtype):
    return jax.ShapeDtypeStruct(shape, dtype)


def cost(flops, nbytes):
    return pl.CostEstimate(flops=flops, bytes_accessed=nbytes, transcendentals=0)


def amp_kernel(sc, own, xa, xb, evc, evr, eo, s_out, w_out, acc, *, half, slot):
    t = pl.program_id(0)

    @pl.when(t == 0)
    def _():
        acc[...] = lax.dot_general(xa[...], own[...], NT, preferred_element_type=F32)

    @pl.when(t == 1)
    def _():
        h = sc[0]
        acc[...] += lax.dot_general(xb[...], own[...], NT, preferred_element_type=F32)
        e = jnp.concatenate([evc[...]] * (half // 128), axis=1)

        def amp(first):
            cols = pl.ds(pl.multiple_of(first * half, half), half)
            return acc[:, cols] / (e + evr[:, cols] - eo[sc[3]] - eo[sc[4 + slot]])

        s_out[...] = amp(1 - h).astype(s_out.dtype)
        mine = amp(h)
        w_out[...] = (2.0 * mine - mine.T).astype(BF16)


def joined(xs):
    first = pl.program_id(0) < pl.num_programs(0) // 2
    return jnp.concatenate([jnp.where(first, xa[...], xb[...]) for xa, xb in xs], axis=0)


def mix(s, q):
    return (2.0 * s[...].astype(F32) - q[...].astype(F32).T).astype(BF16)


def gamma_kernel(sc, *refs, n, half):
    xs = [refs[2 * k : 2 * k + 2] for k in range(n)]
    mixes, outs, w = refs[2 * n : 5 * n], refs[5 * n : 5 * n + 2], refs[5 * n + 2]

    @pl.when(pl.program_id(0) == 0)
    def _():
        for k in range(n):
            s, q, v = mixes[3 * k : 3 * k + 3]
            w[k * half : (k + 1) * half, :half] = v[...]
            w[k * half : (k + 1) * half, half:] = mix(s, q)

    res = lax.dot_general(joined(xs), w[...], TN, preferred_element_type=F32)
    outs[0][...] = res[:, :half]
    outs[1][...] = res[:, half:]


def last_kernel(sc, *refs, n, half, mixed):
    xs = [refs[2 * k : 2 * k + 2] for k in range(n)]
    per = 2 if mixed else 1
    mixes, refs = refs[2 * n : (2 + per) * n], refs[(2 + per) * n :]
    early, keep_far, keep_own, send_far, send_own, w = refs

    @pl.when(pl.program_id(0) == 0)
    def _():
        for k in range(n):
            w[k * half : (k + 1) * half, :] = mix(*mixes[2 * k : 2 * k + 2]) if mixed else mixes[k][...]

    res = early[...] + lax.dot_general(joined(xs), w[...], TN, preferred_element_type=F32)
    res = res.reshape(res.shape[0] // 32, 2, 2, 8, res.shape[1])
    a, b = res[:, :, 0], res[:, :, 1]
    first = sc[1] == 0
    kept, sent = jnp.where(first, a, b), jnp.where(first, b, a)
    first = sc[2] == 0
    keep_far[...] = jnp.where(first, kept[:, 1], kept[:, 0])
    keep_own[...] = jnp.where(first, kept[:, 0], kept[:, 1])
    send_far[...] = jnp.where(first, sent[:, 1], sent[:, 0])
    send_own[...] = jnp.where(first, sent[:, 0], sent[:, 1])


def body(
    factors, occ_level, vir_level, occupied_energy_levels, vir_table, virtual_coefficient_matrix
):
    n_occ = lax.axis_size("occ")
    occ_index = lax.axis_index("occ")
    off_index = lax.axis_index("off")
    chip = off_index // 2
    core = off_index % 2
    own = factors[0]
    n_vir, n_aux = own.shape
    half = n_vir // 2
    h = chip ^ (occ_index // (n_occ // 2))
    partners = [(occ_index - jnp.where(core == 0, a, b)) % n_occ for a, b in ((0, 1), (2, 7), (6, 3), (4, 5))]
    sc = jnp.stack([h, core, chip, occ_index, *partners]).astype(jnp.int32)

    def ring(x, rule):
        return lax.ppermute(x, BOTH, moves(n_occ, rule))

    def exchange(s):
        return lax.ppermute(s, BOTH, swap(n_occ, 2))

    tile = n_aux // 2
    x0 = [lax.dynamic_slice(own, (h * half, p * tile), (half, tile)) for p in range(2)]
    x1 = [ring(x0[p], round1) for p in range(2)]
    x2 = [ring(x1[p], round2) for p in range(2)]

    ev = lookup(vir_level, vir_table)
    eo = lookup(occ_level, occupied_energy_levels)
    evr = ev[None, :]
    evc = jnp.broadcast_to(lax.dynamic_slice_in_dim(ev, h * half, half, 0)[:, None], (half, 128))

    def amp(x, slot, s_dtype):
        return pl.pallas_call(
            functools.partial(amp_kernel, half=half, slot=slot),
            out_shape=(sds((half, half), s_dtype), sds((half, half), BF16)),
            grid_spec=pltpu.PrefetchScalarGridSpec(
                num_scalar_prefetch=1,
                grid=(2,),
                in_specs=[
                    pl.BlockSpec((n_vir, tile), lambda t, s: (0, t)),
                    pl.BlockSpec((half, tile), lambda t, s: (0, 0)),
                    pl.BlockSpec((half, tile), lambda t, s: (0, 0)),
                    pl.BlockSpec((half, 128), lambda t, s: (0, 0)),
                    pl.BlockSpec((1, n_vir), lambda t, s: (0, 0)),
                    pl.BlockSpec(memory_space=pltpu.SMEM),
                ],
                out_specs=[pl.BlockSpec((half, half), lambda t, s: (0, 0))] * 2,
                scratch_shapes=[pltpu.VMEM((half, n_vir), F32)],
            ),
            cost_estimate=cost(2 * n_vir * half * n_aux, 2 * n_aux * (n_vir + half)),
            name="amp",
        )(sc, own, *x, evc, evr, eo)

    tiles = 2
    tile_p = n_aux // tiles
    whole = pl.BlockSpec((half, half), lambda t, s: (0, 0))
    x_specs = [
        pl.BlockSpec((half, tile_p), lambda t, s: (0, jnp.minimum(t, tiles // 2 - 1))),
        pl.BlockSpec((half, tile_p), lambda t, s: (0, jnp.maximum(t - tiles // 2, 0))),
    ]
    row_spec = pl.BlockSpec((tile_p, half), lambda t, s: (t, 0))

    def gamma(xs, mixes):
        n = len(xs)
        return pl.pallas_call(
            functools.partial(gamma_kernel, n=n, half=half),
            out_shape=(sds((n_aux, half), F32),) * 2,
            grid_spec=pltpu.PrefetchScalarGridSpec(
                num_scalar_prefetch=1,
                grid=(tiles,),
                in_specs=x_specs * n + [whole] * (3 * n),
                out_specs=[row_spec] * 2,
                scratch_shapes=[pltpu.VMEM((n * half, n_vir), BF16)],
            ),
            cost_estimate=cost(2 * n * n_aux * half * n_vir, 2 * n * n_aux * half + 4 * n_aux * n_vir),
            name="gamma",
        )(sc, *(a for x in xs for a in x), *(m for mix in mixes for m in mix))

    y1 = [jnp.where(core == 0, x0[p], x1[p]) for p in range(2)]
    s1, v1 = amp(y1, 0, F32)
    q1 = exchange(s1)
    c_halves = virtual_coefficient_matrix.reshape(2, half, -1)
    c_flip = c_halves[::-1]
    c_both = [jnp.concatenate([c[0], c[1]], axis=0) for c in (c_halves, c_flip)]
    c_own = jnp.where(chip == 0, jnp.stack(c_both), jnp.stack(c_both[::-1]))
    x2[0], c_own = lax.optimization_barrier((x2[0], c_own))
    x3 = [ring(x2[p], round3) for p in range(2)]
    s2, v2 = amp(x2, 1, F32)
    q2 = exchange(s2)
    x4 = [ring(x3[p], round4) for p in range(2)]
    s3, v3 = amp(x3, 2, F32)
    q3 = exchange(s3)
    early = gamma([y1, x2], [(s1, q1, v1), (s2, q2, v2)])
    x4[0], _ = lax.optimization_barrier((x4[0], s3))
    x4[1], early = lax.optimization_barrier((x4[1], early))
    s4, v4 = amp(x4, 3, BF16)
    q4 = exchange(s4)

    groups = tile_p // 32

    def last(xs, mixes, early):
        n, mixed = len(xs), len(mixes) == 2 * len(xs)
        return pl.pallas_call(
            functools.partial(last_kernel, n=n, half=half, mixed=mixed),
            out_shape=(sds((n_occ, 8, half), F32),) * 4,
            grid_spec=pltpu.PrefetchScalarGridSpec(
                num_scalar_prefetch=1,
                grid=(tiles,),
                in_specs=x_specs * n + [whole] * len(mixes) + [row_spec],
                out_specs=[pl.BlockSpec((groups, 8, half), lambda t, s: (t, 0, 0))] * 4,
                scratch_shapes=[pltpu.VMEM((n * half, half), BF16)],
            ),
            cost_estimate=cost(n * n_aux * half * n_vir, 2 * n_aux * (n_vir + n * half)),
            name="last",
        )(sc, *(a for x in xs for a in x), *mixes, early)

    def near(x):
        return lax.ppermute(x, BOTH, swap(n_occ, 1))

    def far(keep, got):
        return lax.ppermute((keep + got).astype(BF16), BOTH, swap(n_occ, 2)).astype(F32)

    keep0, own0, send0, mate0 = last([x3, x4], [v3, v4], early[0])
    early1, send0 = lax.optimization_barrier((early[1], send0))
    far0 = far(keep0, near(send0))
    mate0 = near(mate0)
    keep1, own1, send1, mate1 = last([x3, x4], [s3, q3, s4, q4], early1)
    far1 = far(keep1, near(send1))
    mate1 = near(mate1)
    gamma_low = jnp.concatenate(
        [(own0 + mate0 + far1).astype(BF16), (own1 + mate1 + far0).astype(BF16)], axis=2
    )
    mine = lax.all_to_all(gamma_low, "occ", split_axis=0, concat_axis=0, tiled=True)
    mine = mine.reshape(2, n_occ // 2 * mine.shape[1], n_vir)
    out = jnp.einsum("zsd,zdw->zsw", mine, c_own, preferred_element_type=F32)
    return out.reshape(n_occ, -1, out.shape[-1])


def solution(mesh):
    in_specs = (P("occ", None, None), P(), P(), P(), P(), P())
    out_specs = P(None, ("occ", "off"), None)
    return jax.shard_map(body, mesh=mesh, in_specs=in_specs, out_specs=out_specs, check_vma=False)
```

```python
import functools

import jax
import jax.numpy as jnp
from jax import lax
from jax.experimental import pallas as pl
from jax.experimental.pallas import tpu as pltpu
from jax.sharding import PartitionSpec as P


BOTH = ("occ", "off")
F32 = jnp.float32
BF16 = jnp.bfloat16
RING = 8
TN = (((0,), (0,)), ((), ()))
NT = (((1,), (1,)), ((), ()))


def lookup(level, table):
    hits = level[:, None] == jnp.arange(table.shape[0], dtype=jnp.int32)[None, :]
    return jnp.sum(jnp.where(hits, table[None, :], jnp.float32(0.0)), axis=1)


def moves(n_occ, rule):
    pairs = []
    half = n_occ // 2
    for i in range(n_occ):
        for chip in range(2):
            for core in range(2):
                j, to = rule(i, core)
                j %= n_occ
                flip = (i // half) ^ (j // half)
                pairs.append((i * 4 + chip * 2 + core, j * 4 + (chip ^ flip) * 2 + to))
    return pairs


def swap(n_occ, mask):
    return [(i * 4 + o, i * 4 + (o ^ mask)) for i in range(n_occ) for o in range(4)]


def round1(i, core):
    if core == 0:
        return i + 1, 1
    return (i + RING, 0) if i % RING else (i, 0)


def round1_swapped(i, core):
    return round1(i, 1 - core)


def round2(i, core):
    if core == 1:
        return i + 1, 0
    return i - i % RING + (i - 1) % RING, 1


def round3(i, core):
    return (i + 1, 1) if core == 0 else (i - 1, 0)


def round4(i, core):
    return (i + 1, 0) if core == 1 else (i - 1, 1)


def sds(shape, dtype):
    return jax.ShapeDtypeStruct(shape, dtype)


def cost(flops, nbytes):
    return pl.CostEstimate(flops=flops, bytes_accessed=nbytes, transcendentals=0)


def amp_kernel(sc, own, xa, xb, evc, evr, eo, s_out, w_out, acc, *, half, slot):
    t = pl.program_id(0)

    @pl.when(t == 0)
    def _():
        acc[...] = lax.dot_general(xa[...], own[...], NT, preferred_element_type=F32)

    @pl.when(t == 1)
    def _():
        h = sc[0]
        acc[...] += lax.dot_general(xb[...], own[...], NT, preferred_element_type=F32)
        e = jnp.concatenate([evc[...]] * (half // 128), axis=1)

        def amp(first):
            cols = pl.ds(pl.multiple_of(first * half, half), half)
            return acc[:, cols] / (e + evr[:, cols] - eo[sc[3]] - eo[sc[4 + slot]])

        s_out[...] = amp(1 - h).astype(s_out.dtype)
        mine = amp(h)
        w_out[...] = (2.0 * mine - mine.T).astype(BF16)


def joined(xs):
    first = pl.program_id(0) < pl.num_programs(0) // 2
    return jnp.concatenate([jnp.where(first, xa[...], xb[...]) for xa, xb in xs], axis=0)


def mix(s, q):
    return (2.0 * s[...].astype(F32) - q[...].astype(F32).T).astype(BF16)


def gamma_kernel(sc, *refs, n, half):
    xs = [refs[2 * k : 2 * k + 2] for k in range(n)]
    mixes, outs, w = refs[2 * n : 5 * n], refs[5 * n : 5 * n + 2], refs[5 * n + 2]

    @pl.when(pl.program_id(0) == 0)
    def _():
        for k in range(n):
            s, q, v = mixes[3 * k : 3 * k + 3]
            w[k * half : (k + 1) * half, :half] = v[...]
            w[k * half : (k + 1) * half, half:] = mix(s, q)

    res = lax.dot_general(joined(xs), w[...], TN, preferred_element_type=F32)
    outs[0][...] = res[:, :half]
    outs[1][...] = res[:, half:]


def last_kernel(sc, *refs, n, half, mixed):
    xs = [refs[2 * k : 2 * k + 2] for k in range(n)]
    per = 2 if mixed else 1
    mixes, refs = refs[2 * n : (2 + per) * n], refs[(2 + per) * n :]
    early, keep_far, keep_own, send_far, send_own, w = refs

    @pl.when(pl.program_id(0) == 0)
    def _():
        for k in range(n):
            w[k * half : (k + 1) * half, :] = mix(*mixes[2 * k : 2 * k + 2]) if mixed else mixes[k][...]

    res = early[...] + lax.dot_general(joined(xs), w[...], TN, preferred_element_type=F32)
    res = res.reshape(res.shape[0] // 32, 2, 2, 8, res.shape[1])
    a, b = res[:, :, 0], res[:, :, 1]
    first = sc[1] == 0
    kept, sent = jnp.where(first, a, b), jnp.where(first, b, a)
    first = sc[2] == 0
    keep_far[...] = jnp.where(first, kept[:, 1], kept[:, 0])
    keep_own[...] = jnp.where(first, kept[:, 0], kept[:, 1])
    send_far[...] = jnp.where(first, sent[:, 1], sent[:, 0])
    send_own[...] = jnp.where(first, sent[:, 0], sent[:, 1])


def body(
    factors, occ_level, vir_level, occupied_energy_levels, vir_table, virtual_coefficient_matrix
):
    n_occ = lax.axis_size("occ")
    occ_index = lax.axis_index("occ")
    off_index = lax.axis_index("off")
    chip = off_index // 2
    core = off_index % 2
    own = factors[0]
    n_vir, n_aux = own.shape
    half = n_vir // 2
    h = chip ^ (occ_index // (n_occ // 2))
    partners = [(occ_index - jnp.where(core == 0, a, b)) % n_occ for a, b in ((0, 1), (2, 7), (6, 3), (4, 5))]
    sc = jnp.stack([h, core, chip, occ_index, *partners]).astype(jnp.int32)

    def ring(x, rule):
        return lax.ppermute(x, BOTH, moves(n_occ, rule))

    def exchange(s):
        return lax.ppermute(s, BOTH, swap(n_occ, 2))

    tile = n_aux // 2
    x0 = [lax.dynamic_slice(own, (h * half, p * tile), (half, tile)) for p in range(2)]
    x1 = [ring(x0[p], rule) for p, rule in enumerate((round1, round1_swapped))]
    x2 = [ring(x1[p], round2) for p in range(2)]

    ev = lookup(vir_level, vir_table)
    eo = lookup(occ_level, occupied_energy_levels)
    evr = ev[None, :]
    evc = jnp.broadcast_to(lax.dynamic_slice_in_dim(ev, h * half, half, 0)[:, None], (half, 128))

    def amp(x, slot, s_dtype):
        return pl.pallas_call(
            functools.partial(amp_kernel, half=half, slot=slot),
            out_shape=(sds((half, half), s_dtype), sds((half, half), BF16)),
            grid_spec=pltpu.PrefetchScalarGridSpec(
                num_scalar_prefetch=1,
                grid=(2,),
                in_specs=[
                    pl.BlockSpec((n_vir, tile), lambda t, s: (0, t)),
                    pl.BlockSpec((half, tile), lambda t, s: (0, 0)),
                    pl.BlockSpec((half, tile), lambda t, s: (0, 0)),
                    pl.BlockSpec((half, 128), lambda t, s: (0, 0)),
                    pl.BlockSpec((1, n_vir), lambda t, s: (0, 0)),
                    pl.BlockSpec(memory_space=pltpu.SMEM),
                ],
                out_specs=[pl.BlockSpec((half, half), lambda t, s: (0, 0))] * 2,
                scratch_shapes=[pltpu.VMEM((half, n_vir), F32)],
            ),
            cost_estimate=cost(2 * n_vir * half * n_aux, 2 * n_aux * (n_vir + half)),
            name="amp",
        )(sc, own, *x, evc, evr, eo)

    tiles = 2
    tile_p = n_aux // tiles
    whole = pl.BlockSpec((half, half), lambda t, s: (0, 0))
    x_specs = [
        pl.BlockSpec((half, tile_p), lambda t, s: (0, jnp.minimum(t, tiles // 2 - 1))),
        pl.BlockSpec((half, tile_p), lambda t, s: (0, jnp.maximum(t - tiles // 2, 0))),
    ]
    row_spec = pl.BlockSpec((tile_p, half), lambda t, s: (t, 0))

    def gamma(xs, mixes):
        n = len(xs)
        return pl.pallas_call(
            functools.partial(gamma_kernel, n=n, half=half),
            out_shape=(sds((n_aux, half), F32),) * 2,
            grid_spec=pltpu.PrefetchScalarGridSpec(
                num_scalar_prefetch=1,
                grid=(tiles,),
                in_specs=x_specs * n + [whole] * (3 * n),
                out_specs=[row_spec] * 2,
                scratch_shapes=[pltpu.VMEM((n * half, n_vir), BF16)],
            ),
            cost_estimate=cost(2 * n * n_aux * half * n_vir, 2 * n * n_aux * half + 4 * n_aux * n_vir),
            name="gamma",
        )(sc, *(a for x in xs for a in x), *(m for mix in mixes for m in mix))

    y1 = [jnp.where(core == 0, x0[p], x1[p]) for p in range(2)]
    s1, v1 = amp(y1, 0, F32)
    q1 = exchange(s1)
    c_halves = virtual_coefficient_matrix.reshape(2, half, -1)
    c_flip = c_halves[::-1]
    c_both = [jnp.concatenate([c[0], c[1]], axis=0) for c in (c_halves, c_flip)]
    c_own = jnp.where(chip == 0, jnp.stack(c_both), jnp.stack(c_both[::-1]))
    x3 = [ring(x2[p], round3) for p in range(2)]
    s2, v2 = amp(x2, 1, F32)
    q2 = exchange(s2)
    x3[1], c_own = lax.optimization_barrier((x3[1], c_own))
    x4 = [ring(x3[p], round4) for p in range(2)]
    s3, v3 = amp(x3, 2, F32)
    q3 = exchange(s3)
    early = gamma([y1, x2], [(s1, q1, v1), (s2, q2, v2)])
    x4[0], _ = lax.optimization_barrier((x4[0], s3))
    x4[1], early = lax.optimization_barrier((x4[1], early))
    s4, v4 = amp(x4, 3, BF16)
    q4 = exchange(s4)

    groups = tile_p // 32

    def last(xs, mixes, early):
        n, mixed = len(xs), len(mixes) == 2 * len(xs)
        return pl.pallas_call(
            functools.partial(last_kernel, n=n, half=half, mixed=mixed),
            out_shape=(sds((n_occ, 8, half), F32),) * 4,
            grid_spec=pltpu.PrefetchScalarGridSpec(
                num_scalar_prefetch=1,
                grid=(tiles,),
                in_specs=x_specs * n + [whole] * len(mixes) + [row_spec],
                out_specs=[pl.BlockSpec((groups, 8, half), lambda t, s: (t, 0, 0))] * 4,
                scratch_shapes=[pltpu.VMEM((n * half, half), BF16)],
            ),
            cost_estimate=cost(n * n_aux * half * n_vir, 2 * n_aux * (n_vir + n * half)),
            name="last",
        )(sc, *(a for x in xs for a in x), *mixes, early)

    def near(x):
        return lax.ppermute(x, BOTH, swap(n_occ, 1))

    def far(keep, got):
        return lax.ppermute((keep + got).astype(BF16), BOTH, swap(n_occ, 2)).astype(F32)

    keep0, own0, send0, mate0 = last([x3, x4], [v3, v4], early[0])
    early1, send0 = lax.optimization_barrier((early[1], send0))
    far0 = far(keep0, near(send0))
    mate0 = near(mate0)
    keep1, own1, send1, mate1 = last([x3, x4], [s3, q3, s4, q4], early1)
    far1 = far(keep1, near(send1))
    mate1 = near(mate1)
    gamma_low = jnp.concatenate(
        [(own0 + mate0 + far1).astype(BF16), (own1 + mate1 + far0).astype(BF16)], axis=2
    )
    mine = lax.all_to_all(gamma_low, "occ", split_axis=0, concat_axis=0, tiled=True)
    mine = mine.reshape(2, n_occ // 2 * mine.shape[1], n_vir)
    out = jnp.einsum("zsd,zdw->zsw", mine, c_own, preferred_element_type=F32)
    return out.reshape(n_occ, -1, out.shape[-1])


def solution(mesh):
    in_specs = (P("occ", None, None), P(), P(), P(), P(), P())
    out_specs = P(None, ("occ", "off"), None)
    return jax.shard_map(body, mesh=mesh, in_specs=in_specs, out_specs=out_specs, check_vma=False)
```
